32 devices in a mesh: dp: 16 (over z, y, core), tensor: 2 (over x).
Axes of the slice: x: 2, y: 2, z: 4, core: 2. Of those that a mesh axis runs over, the one named last changes fastest.
Arguments:
- tokens: bfloat16 [16384, 768], P(('dp', 'tensor')), may hold values from -6 to 6
- query_weight: bfloat16 [768, 768], P('dp', 'tensor'), may hold values from -0.21875 to 0.21875
- query_bias: float32 [768], replicated, may hold values from -3 to 3
- key_weight: bfloat16 [768, 768], P('dp', 'tensor'), may hold values from -0.21875 to 0.21875
- value_weight: bfloat16 [768, 768], P('dp', 'tensor'), may hold values from -0.21875 to 0.21875
- value_bias: float32 [768], replicated, may hold values from -0.625 to 0.625
- output_weight: bfloat16 [768, 768], P('tensor', 'dp'), may hold values from -1.25 to 1.25
- output_bias: float32 [768], replicated, may hold values from -3 to 3
- first_gain: float32 [768], replicated, may hold values from 0.5 to 1.5
- first_shift: float32 [768], replicated, may hold values from -3 to 3
- inner_weight: bfloat16 [768, 3072], P('dp', 'tensor'), may hold values from -0.21875 to 0.21875
- inner_bias: float32 [3072], replicated, may hold values from -3 to 3
- outer_weight: bfloat16 [3072, 768], P('tensor', 'dp'), may hold values from -0.109375 to 0.109375
- outer_bias: float32 [768], replicated, may hold values from -3 to 3
- second_gain: float32 [768], replicated, may hold values from 0.5 to 1.5
- second_shift: float32 [768], replicated, may hold values from -3 to 3
- segments: int32 [16, 1024], P('dp'), may hold values from 0 to 7, never falling along the last dimension, each value on 1 to 768 neighbouring positions
- valid_length: int32 [16], P('dp'), may hold values from 512 to 1024
- cotangent: bfloat16 [16384, 768], P(('dp', 'tensor')), may hold values from -6 to 6
Outputs:
- layer_output: bfloat16 [16384, 768], P(('dp', 'tensor'))
- input_gradient: float32 [16384, 768], P(('dp', 'tensor'))
- query_weight_gradient: float32 [768, 768], P('dp', 'tensor')
- query_bias_gradient: float32 [768], replicated
- key_weight_gradient: float32 [768, 768], P('dp', 'tensor')
- value_weight_gradient: float32 [768, 768], P('dp', 'tensor')
- value_bias_gradient: float32 [768], replicated
- output_weight_gradient: float32 [768, 768], P('tensor', 'dp')
- output_bias_gradient: float32 [768], replicated
- first_gain_gradient: float32 [768], replicated
- first_shift_gradient: float32 [768], replicated
- inner_weight_gradient: float32 [768, 3072], P('dp', 'tensor')
- inner_bias_gradient: float32 [3072], replicated
- outer_weight_gradient: float32 [3072, 768], P('tensor', 'dp')
- outer_bias_gradient: float32 [768], replicated
- second_gain_gradient: float32 [768], replicated
- second_shift_gradient: float32 [768], replicated
The draws below stay inside these ranges and needn't reach their ends.
Inputs may be any that keep to these rules, and one draw needn't show every extreme that they name: `segments`: segment numbers never fall along a sequence; a token attends only to tokens of its own document. tokens of a sequence at positions valid_length and beyond are padding: no query attends to them as keys except the token itself.
All inputs are finite; a program needn't handle non-finite values.
Results may differ from the reference program's by a relative error of at most 0.013.
Values may be sent and summed in bfloat16 or wider, within the bound.
No kernel may reach another device: no remote copies, remote signals or barrier semaphores. Data moves between devices by JAX's collectives and lax.ppermute only.
A program may use at most 128 MiB of HBM per device.

```python
import math
import jax
import jax.numpy as jnp
import numpy as np
from jax import lax

D = 768
HEADS = 12
HEAD_DIM = 64
FF = 3072
SEQ_LEN = 1024
SEQS = 16
TOKENS = 16384


def place_ends(array, stream_key, smallest, high):
    spot = [jax.random.randint(jax.random.fold_in(stream_key, axis), (), 0, length) for axis, length in enumerate(array.shape)]
    widest = array.shape.index(max(array.shape))
    next_to = spot[:widest] + [(spot[widest] + 1) % array.shape[widest]] + spot[widest + 1:]
    return array.at[tuple(spot)].set(smallest).at[tuple(next_to)].set(high)


def with_spikes(entries, key, source, target, shards_of, factor):
    owner, partner = [(jnp.arange(entries.shape[axis_at]) // (entries.shape[axis_at] // shards_of)).reshape([-1 if axis == axis_at else 1 for axis in range(entries.ndim)]) for axis_at in (source, target)]
    chosen = jax.random.permutation(key, shards_of)[partner]
    strong = (owner == chosen) | (owner == (partner + shards_of // 2) % shards_of)
    return jnp.where(strong, factor * entries, entries)


def levels(rng, dims, shards, low, top_value):
    def one(position, parts):
        steps = jax.random.uniform(jax.random.fold_in(jax.random.fold_in(rng, 6), position), (parts,), jnp.float32, low / len(shards), top_value / len(shards))
        return jnp.repeat(jnp.exp(steps), dims[position] // parts).reshape((-1,) + (1,) * (len(dims) - position - 1))

    level = one(*shards[0])
    for cut in shards[1:]:
        level = level * one(*cut)
    return level


def profile(amount, total, reach, slope):
    weights = [(1 << 20) // math.isqrt(standing ** slope) + 1 for standing in range(2, amount + 1)]
    surplus, holding = total - reach - (amount - 1), [1] * (amount - 1)
    while surplus > 0:
        free = [i for i in range(amount - 1) if holding[i] < reach]
        pool, budget = sum([weights[i] for i in free]), surplus
        for i in free:
            extra = min(reach - holding[i], max(1, budget * weights[i] // pool), surplus)
            holding[i] = holding[i] + extra
            surplus = surplus - extra
    return np.array([reach] + holding)


def ragged(own_key, count, total, bound, slope):
    if count == 2:
        one = jax.random.randint(own_key, (), max(1, total - bound), min(bound, total - 1) + 1)
        return jnp.stack([one, total - one])
    tallies = jnp.asarray(profile(count, total, bound, slope), jnp.int32)
    couples = (count - 1) // 2
    source_of, receiver = tallies[1:1 + 2 * couples:2], tallies[2:2 + 2 * couples:2]
    margin = jnp.minimum(source_of - 1, bound - receiver)
    shifted = jax.random.randint(jax.random.fold_in(own_key, 1), (couples,), 0, 1 << 20) % (margin + 1)
    tallies = tallies.at[1:1 + 2 * couples:2].set(source_of - shifted).at[2:2 + 2 * couples:2].set(receiver + shifted)
    return tallies[jax.random.permutation(jax.random.fold_in(own_key, 2), count)]


def scatter_about(rng, shape, width, reach, cuts=(), kind=jnp.bfloat16):
    values = width * jax.random.normal(rng, shape, jnp.float32)
    if cuts:
        values = values * levels(rng, shape, cuts, -0.22, 0.18)
    return jnp.clip(values, -reach, reach).astype(kind)


def noise_with(stream_key, dims, scale, reach, cuts, heavy, kind=jnp.bfloat16):
    array = scale * jax.random.normal(stream_key, dims, jnp.float32)
    if cuts:
        array = array * levels(stream_key, dims, cuts, -0.22, 0.18)
    return jnp.clip(with_spikes(array, jax.random.fold_in(stream_key, 3), *heavy), -reach, reach).astype(kind)


def setup_inputs(seed: int = 0) -> dict:
    streams_of = jax.random.split(jax.random.key(seed), 20)
    tokens = noise_with(streams_of[0], (TOKENS, D), 1.0, 6.0, ((0, 32),), (0, 1, 32, 2.75))
    query_weight = scatter_about(streams_of[1], (D, D), D ** -0.5, 0.21875, ((0, 16), (1, 2)))
    query_bias = scatter_about(streams_of[2], (D,), 0.5, 3.0, (), jnp.float32)
    key_weight = scatter_about(streams_of[3], (D, D), D ** -0.5, 0.21875, ((0, 16), (1, 2)))
    value_weight = scatter_about(streams_of[4], (D, D), D ** -0.5, 0.21875, ((0, 16), (1, 2)))
    value_bias = scatter_about(streams_of[5], (D,), 0.1, 0.625, (), jnp.float32)
    output_weight = scatter_about(streams_of[6], (D, D), (D // 32) ** -0.5, 1.25, ((0, 2), (1, 16)))
    output_bias = scatter_about(streams_of[7], (D,), 0.5, 3.0, (), jnp.float32)
    first_gain = jnp.clip(1.0 + 0.1 * jax.random.normal(streams_of[8], (D,), jnp.float32), 0.5, 1.5)
    first_shift = scatter_about(streams_of[9], (D,), 0.5, 3.0, (), jnp.float32)
    inner_weight = scatter_about(streams_of[10], (D, FF), D ** -0.5, 0.21875, ((0, 16), (1, 2)))
    inner_bias = scatter_about(streams_of[11], (FF,), 0.5, 3.0, (), jnp.float32)
    outer_weight = scatter_about(streams_of[12], (FF, D), FF ** -0.5, 0.109375, ((0, 2), (1, 16)))
    outer_bias = scatter_about(streams_of[13], (D,), 0.5, 3.0, (), jnp.float32)
    second_gain = jnp.clip(1.0 + 0.1 * jax.random.normal(streams_of[14], (D,), jnp.float32), 0.5, 1.5)
    second_shift = scatter_about(streams_of[15], (D,), 0.5, 3.0, (), jnp.float32)
    segments = jax.vmap(lambda own: jnp.searchsorted(jnp.cumsum(ragged(own, max(4, SEQ_LEN // 128), SEQ_LEN, 3 * SEQ_LEN // 4, 2)), jnp.arange(SEQ_LEN), side="right"))(jax.random.split(streams_of[16], SEQS)).reshape((SEQS, SEQ_LEN)).astype(jnp.int32)
    valid_length = place_ends(jax.random.randint(streams_of[17], (SEQS,), SEQ_LEN // 2, SEQ_LEN + 1), jax.random.fold_in(streams_of[17], 1), SEQ_LEN // 2, SEQ_LEN).astype(jnp.int32)
    cotangent = scatter_about(streams_of[18], (TOKENS, D), 1.0, 6.0, ((0, 32),))
    return dict(tokens=tokens, query_weight=query_weight, query_bias=query_bias, key_weight=key_weight, value_weight=value_weight, value_bias=value_bias, output_weight=output_weight, output_bias=output_bias, first_gain=first_gain, first_shift=first_shift, inner_weight=inner_weight, inner_bias=inner_bias, outer_weight=outer_weight, outer_bias=outer_bias, second_gain=second_gain, second_shift=second_shift, segments=segments, valid_length=valid_length, cotangent=cotangent)


@jax.custom_vjp
def low(v):
    return lax.optimization_barrier(v.astype(jnp.bfloat16)).astype(jnp.float32)

@jax.custom_vjp
def low_back(v):
    return v

def low_keep(v):
    return (low(v), None)

def low_pass(kept, grad):
    return (grad,)

def back_keep(v):
    return (v, None)

def back_low(kept, grad):
    return (low(grad),)
low.defvjp(low_keep, low_pass)
low_back.defvjp(back_keep, back_low)
norm_epsilon = 1e-12
masked_score = -1e+30

def matmul(left, right):
    return jnp.dot(left, right, precision=lax.Precision.HIGHEST)

def normalize(matrix, gain, shift):
    center = matrix - lax.optimization_barrier(jnp.mean(matrix, axis=-1, keepdims=True))
    spread = lax.optimization_barrier(jnp.mean(center * center, axis=-1, keepdims=True))
    return center * lax.rsqrt(spread + norm_epsilon) * gain + shift

def attend(pieces):
    queries, keys_all, values_all, segment_row, valid_count = pieces
    length = queries.shape[0]
    scores = jnp.einsum('qhd,khd->hqk', queries, keys_all, precision=lax.Precision.HIGHEST) * 0.125
    scores = low_back(scores)
    positions = jnp.arange(length, dtype=jnp.int32)
    allowed = (segment_row[:, None] == segment_row[None, :]) & ((positions[None, :] < valid_count) | (positions[:, None] == positions[None, :]))
    masked = jnp.where(allowed[None], scores, masked_score)
    largest = lax.optimization_barrier(jnp.max(masked, axis=-1, keepdims=True))
    totals = lax.optimization_barrier(jnp.sum(jnp.exp(masked - largest), axis=-1, keepdims=True))
    probs = low(jnp.exp(masked - (largest + jnp.log(totals))))
    return jnp.einsum('hqk,khd->qhd', probs, values_all, precision=lax.Precision.HIGHEST)

def layer(tokens, query_weight, query_bias, key_weight, value_weight, value_bias, output_weight, output_bias, first_gain, first_shift, inner_weight, inner_bias, outer_weight, outer_bias, second_gain, second_shift, segments, valid_length):
    queries = low(low_back(matmul(tokens, query_weight) + query_bias))
    keys_all = low(low_back(matmul(tokens, key_weight)))
    values_all = low(low_back(matmul(tokens, value_weight) + value_bias))
    four_shape = (SEQS, SEQ_LEN, HEADS, HEAD_DIM)
    context = lax.map(jax.checkpoint(attend), (queries.reshape(four_shape), keys_all.reshape(four_shape), values_all.reshape(four_shape), segments, valid_length))
    context = low(low_back(context.reshape(TOKENS, D)))
    attended = low_back(matmul(context, output_weight)) + output_bias
    hidden = normalize(tokens + attended, first_gain, first_shift)
    inner = low_back(matmul(low(hidden), inner_weight) + inner_bias)
    activated = low(jax.nn.gelu(inner, approximate=False))
    outer = low_back(matmul(activated, outer_weight)) + outer_bias
    return normalize(hidden + outer, second_gain, second_shift)

def reference(tokens, query_weight, query_bias, key_weight, value_weight, value_bias, output_weight, output_bias, first_gain, first_shift, inner_weight, inner_bias, outer_weight, outer_bias, second_gain, second_shift, segments, valid_length, cotangent):

    def forward(tokens_f, query_w, query_b, key_w, value_w, value_b, output_w, output_b, gain_one, shift_one, inner_w, inner_b, outer_w, outer_b, gain_two, shift_two):
        return layer(tokens_f, query_w, query_b, key_w, value_w, value_b, output_w, output_b, gain_one, shift_one, inner_w, inner_b, outer_w, outer_b, gain_two, shift_two, segments, valid_length)
    final, pullback = jax.vjp(forward, tokens.astype(jnp.float32), query_weight.astype(jnp.float32), query_bias.astype(jnp.float32), key_weight.astype(jnp.float32), value_weight.astype(jnp.float32), value_bias.astype(jnp.float32), output_weight.astype(jnp.float32), output_bias.astype(jnp.float32), first_gain.astype(jnp.float32), first_shift.astype(jnp.float32), inner_weight.astype(jnp.float32), inner_bias.astype(jnp.float32), outer_weight.astype(jnp.float32), outer_bias.astype(jnp.float32), second_gain.astype(jnp.float32), second_shift.astype(jnp.float32))
    grads = pullback(cotangent.astype(jnp.float32))
    return (final.astype(jnp.bfloat16), grads[0], grads[1], grads[2], grads[3], grads[4], grads[5], grads[6], grads[7], grads[8], grads[9], grads[10], grads[11], grads[12], grads[13], grads[14], grads[15])
```

```python
import jax
import jax.numpy as jnp
from jax import lax
from jax.sharding import PartitionSpec as P

HEAD_DIM = 64


norm_epsilon = 1e-12
masked_score = -1e30


def normalize(matrix, gain, shift):
    center = matrix - jnp.mean(matrix, axis=-1, keepdims=True)
    spread = jnp.mean(center * center, axis=-1, keepdims=True)
    return center * lax.rsqrt(spread + norm_epsilon) * gain + shift


def block_scores(query_block, key_seq, segment_row, valid_count, first_row):
    block_rows = query_block.shape[0]
    length = key_seq.shape[0]
    scores = (
        jnp.einsum("qhd,khd->hqk", query_block, key_seq, preferred_element_type=jnp.float32) * 0.125
    )
    positions = jnp.arange(length, dtype=jnp.int32)
    query_pos = first_row + jnp.arange(block_rows, dtype=jnp.int32)
    query_seg = lax.dynamic_slice_in_dim(segment_row, first_row, block_rows)
    allowed = (query_seg[:, None] == segment_row[None, :]) & (
        (positions[None, :] < valid_count) | (query_pos[:, None] == positions[None, :])
    )
    return jnp.where(allowed[None], scores, masked_score)


def attend_sequence(pieces):
    query_seq, key_seq, value_seq, segment_row, valid_count = pieces
    length = query_seq.shape[0]
    block_rows = min(512, length)

    def one_block(block_index):
        first_row = block_index * block_rows
        query_block = lax.dynamic_slice_in_dim(query_seq, first_row, block_rows)
        masked = block_scores(query_block, key_seq, segment_row, valid_count, first_row)
        largest = jnp.max(masked, axis=-1, keepdims=True)
        totals = jnp.sum(jnp.exp(masked - largest), axis=-1, keepdims=True)
        log_total = largest + jnp.log(totals)
        probs_low = jnp.exp(masked - log_total).astype(jnp.bfloat16)
        context = jnp.einsum(
            "hqk,khd->qhd", probs_low, value_seq, preferred_element_type=jnp.float32
        )
        return (context.astype(jnp.bfloat16), log_total[..., 0])

    contexts, log_totals = lax.map(one_block, jnp.arange(length // block_rows, dtype=jnp.int32))
    return (contexts.reshape(query_seq.shape), log_totals)


def attend_backward(pieces):
    query_seq, key_seq, value_seq, segment_row, valid_count, grad_seq, log_totals = pieces
    length = query_seq.shape[0]
    block_rows = min(512, length)

    def one_block(running, inputs):
        key_grad, value_grad = running
        block_index, log_total = inputs
        first_row = block_index * block_rows
        query_block = lax.dynamic_slice_in_dim(query_seq, first_row, block_rows)
        grad_block = lax.dynamic_slice_in_dim(grad_seq, first_row, block_rows)
        masked = block_scores(query_block, key_seq, segment_row, valid_count, first_row)
        probs = jnp.exp(masked - log_total[..., None])
        probs_low = probs.astype(jnp.bfloat16)
        value_grad = value_grad + jnp.einsum(
            "hqk,qhd->khd", probs_low, grad_block, preferred_element_type=jnp.float32
        )
        d_probs = jnp.einsum(
            "qhd,khd->hqk", grad_block, value_seq, preferred_element_type=jnp.float32
        )
        row_inner = jnp.sum(probs * d_probs, axis=-1, keepdims=True)
        d_scores = (probs * (d_probs - row_inner)).astype(jnp.bfloat16)
        query_grad = (
            jnp.einsum("hqk,khd->qhd", d_scores, key_seq, preferred_element_type=jnp.float32)
            * 0.125
        )
        key_grad = (
            key_grad
            + jnp.einsum("hqk,qhd->khd", d_scores, query_block, preferred_element_type=jnp.float32)
            * 0.125
        )
        return ((key_grad, value_grad), query_grad.astype(jnp.bfloat16))

    empty = jnp.zeros(key_seq.shape, jnp.float32)
    block_ids = jnp.arange(length // block_rows, dtype=jnp.int32)
    (key_grad, value_grad), query_grads = lax.scan(
        one_block, (empty, empty), (block_ids, log_totals)
    )
    return (
        query_grads.reshape(query_seq.shape),
        key_grad.astype(jnp.bfloat16),
        value_grad.astype(jnp.bfloat16),
    )


def slope_and_gelu(inner):
    rise = 0.5 * (1.0 + lax.erf(inner * 0.7071067811865476))
    density = jnp.exp(-0.5 * inner * inner) * 0.3989422804014327
    return inner * rise, rise + inner * density


def norm_backward(matrix, gain, grad):
    center = matrix - jnp.mean(matrix, axis=-1, keepdims=True)
    spread = jnp.mean(center * center, axis=-1, keepdims=True)
    scale = lax.rsqrt(spread + norm_epsilon)
    normed = center * scale
    d_normed = grad * gain
    pulled = scale * (
        d_normed
        - jnp.mean(d_normed, axis=-1, keepdims=True)
        - normed * jnp.mean(d_normed * normed, axis=-1, keepdims=True)
    )
    return pulled, jnp.sum(grad * normed, axis=0), jnp.sum(grad, axis=0)


def halves_in_order(mine, other, shard_index):
    first = shard_index == 0
    return jnp.where(first, mine, other), jnp.where(first, other, mine)


def mix(left, right, dims):
    return lax.dot_general(left, right, (dims, ((), ())), preferred_element_type=jnp.float32)


def on_device(
    tokens,
    query_weight,
    query_bias,
    key_weight,
    value_weight,
    value_bias,
    output_weight,
    output_bias,
    first_gain,
    first_shift,
    inner_weight,
    inner_bias,
    outer_weight,
    outer_bias,
    second_gain,
    second_shift,
    segments,
    valid_length,
    cotangent,
):
    low = jnp.bfloat16
    whole = ("tensor", "dp")
    swap = [(0, 1), (1, 0)]
    own_rows, width = tokens.shape
    head_cols = query_weight.shape[1]
    hidden_cols = inner_weight.shape[1]
    local_heads = head_cols // HEAD_DIM
    shard_index = lax.axis_index("tensor")
    own_start = shard_index * own_rows
    other_start = (1 - shard_index) * own_rows

    other_tokens = lax.ppermute(tokens, "tensor", swap)
    full_qkv = lax.all_gather(
        jnp.concatenate([query_weight, key_weight, value_weight], axis=1), "dp", axis=0, tiled=True
    )
    full_output = lax.all_gather(output_weight.T, whole, axis=0, tiled=True)
    full_inner = lax.all_gather(inner_weight, whole, axis=0, tiled=True)
    full_outer = lax.all_gather(outer_weight.T, whole, axis=0, tiled=True)
    full_output = full_output.reshape(2, width, head_cols)
    full_inner = full_inner.reshape(2, width, hidden_cols)
    full_outer = full_outer.reshape(2, width, hidden_cols)

    group_rows = jnp.concatenate(halves_in_order(tokens, other_tokens, shard_index), axis=0)
    bias_query = lax.dynamic_slice_in_dim(query_bias, shard_index * head_cols, head_cols)
    bias_value = lax.dynamic_slice_in_dim(value_bias, shard_index * head_cols, head_cols)
    bias_qkv = jnp.concatenate([bias_query, jnp.zeros_like(bias_query), bias_value])
    seq_count, seq_length = segments.shape
    four_shape = (seq_count, seq_length, local_heads, HEAD_DIM)
    qkv = (mix(group_rows, full_qkv, ((1,), (0,))) + bias_qkv).astype(low)
    queries = qkv[:, :head_cols].reshape(four_shape)
    keys_all = qkv[:, head_cols : 2 * head_cols].reshape(four_shape)
    values_all = qkv[:, 2 * head_cols :].reshape(four_shape)
    contexts, log_totals = lax.map(
        attend_sequence, (queries, keys_all, values_all, segments, valid_length)
    )
    context = contexts.reshape(seq_count * seq_length, head_cols)
    own_context = lax.dynamic_slice_in_dim(context, own_start, own_rows)
    far_context = lax.ppermute(
        lax.dynamic_slice_in_dim(context, other_start, own_rows), "tensor", swap
    )
    context_halves = halves_in_order(own_context, far_context, shard_index)
    attended = mix(context_halves[0], full_output[0], ((1,), (1,))) + mix(
        context_halves[1], full_output[1], ((1,), (1,))
    )
    first_sum = tokens.astype(jnp.float32) + attended + output_bias
    hidden = normalize(first_sum, first_gain, first_shift)
    hidden_low = hidden.astype(low)
    activated, slopes = [], []
    outer = outer_bias
    for half in range(2):
        inner = (
            mix(hidden_low, full_inner[half], ((1,), (0,)))
            + inner_bias[half * hidden_cols : (half + 1) * hidden_cols]
        )
        value, slope = slope_and_gelu(inner)
        activated.append(value.astype(low))
        slopes.append(slope)
        outer = outer + mix(activated[half], full_outer[half], ((1,), (1,)))
    second_sum = hidden + outer
    layer_output = normalize(second_sum, second_gain, second_shift).astype(low)
    d_second, second_gain_grad, second_shift_grad = norm_backward(
        second_sum, second_gain, cotangent.astype(jnp.float32)
    )
    outer_bias_grad = jnp.sum(d_second, axis=0)
    d_outer = d_second.astype(low)
    outer_weight_grad = jnp.stack(
        [mix(d_outer, activated[half], ((0,), (0,))).astype(low) for half in range(2)]
    )
    d_hidden = d_second
    inner_grads, inner_bias_parts = [], []
    for half in range(2):
        d_activated = mix(d_outer, full_outer[half], ((1,), (0,)))
        d_inner = (d_activated * slopes[half]).astype(low)
        inner_grads.append(mix(hidden_low, d_inner, ((0,), (0,))).astype(low))
        inner_bias_parts.append(jnp.sum(d_inner, axis=0, dtype=jnp.float32))
        d_hidden = d_hidden + mix(d_inner, full_inner[half], ((1,), (1,)))
    inner_weight_grad = jnp.stack(inner_grads)
    inner_bias_grad = jnp.concatenate(inner_bias_parts)
    d_first, first_gain_grad, first_shift_grad = norm_backward(first_sum, first_gain, d_hidden)
    output_bias_grad = jnp.sum(d_first, axis=0)
    d_attended = d_first.astype(low)
    output_weight_grad = jnp.stack(
        [mix(d_attended, context_halves[half], ((0,), (0,))).astype(low) for half in range(2)]
    )
    d_context_halves = [
        mix(d_attended, full_output[half], ((1,), (0,))).astype(low) for half in range(2)
    ]
    first = shard_index == 0
    own_d_context = jnp.where(first, d_context_halves[0], d_context_halves[1])
    far_d_context = lax.ppermute(
        jnp.where(first, d_context_halves[1], d_context_halves[0]), "tensor", swap
    )
    d_context = jnp.concatenate(
        halves_in_order(own_d_context, far_d_context, shard_index), axis=0
    )
    d_queries, d_keys, d_values = lax.map(
        attend_backward,
        (
            queries,
            keys_all,
            values_all,
            segments,
            valid_length,
            d_context.reshape(four_shape),
            log_totals,
        ),
    )
    flat = (seq_count * seq_length, head_cols)
    d_qkv = jnp.concatenate(
        [d_queries.reshape(flat), d_keys.reshape(flat), d_values.reshape(flat)], axis=1
    )
    qkv_weight_grad = mix(group_rows, d_qkv, ((0,), (0,))).astype(low)
    partial_input = mix(d_qkv, full_qkv, ((1,), (1,)))
    far_input = lax.ppermute(
        lax.dynamic_slice_in_dim(partial_input, other_start, own_rows).astype(low), "tensor", swap
    )
    input_gradient = (
        d_first
        + lax.dynamic_slice_in_dim(partial_input, own_start, own_rows)
        + far_input.astype(jnp.float32)
    )

    def scatter(partial, axes):
        return lax.psum_scatter(
            partial.reshape(-1, partial.shape[-1]), axes, scatter_dimension=0, tiled=True
        ).astype(jnp.float32)

    outer_shard = scatter(outer_weight_grad, whole).T
    inner_shard = scatter(inner_weight_grad, whole)
    output_shard = scatter(output_weight_grad, whole).T
    qkv_shard = scatter(qkv_weight_grad, ("dp",))
    bias_local = jnp.sum(d_qkv, axis=0, dtype=jnp.float32)
    spread_out = lax.dynamic_update_slice(
        jnp.zeros((2, width), jnp.float32),
        jnp.stack([bias_local[:head_cols], bias_local[2 * head_cols :]]),
        (0, shard_index * head_cols),
    )
    pieces = [
        spread_out.reshape(-1),
        output_bias_grad,
        first_gain_grad,
        first_shift_grad,
        outer_bias_grad,
        second_gain_grad,
        second_shift_grad,
        inner_bias_grad,
    ]
    summed = lax.psum(jnp.concatenate(pieces), ("dp", "tensor"))
    rows = summed[: 8 * width].reshape(8, width)
    return (
        layer_output,
        input_gradient,
        qkv_shard[:, :head_cols],
        rows[0],
        qkv_shard[:, head_cols : 2 * head_cols],
        qkv_shard[:, 2 * head_cols :],
        rows[1],
        output_shard,
        rows[2],
        rows[3],
        rows[4],
        inner_shard,
        summed[8 * width :],
        outer_shard,
        rows[5],
        rows[6],
        rows[7],
    )


def solution(mesh):
    placed = (
        P(("dp", "tensor"), None),
        P("dp", "tensor"),
        P(),
        P("dp", "tensor"),
        P("dp", "tensor"),
        P(),
        P("tensor", "dp"),
        P(),
        P(),
        P(),
        P("dp", "tensor"),
        P(),
        P("tensor", "dp"),
        P(),
        P(),
        P(),
        P("dp", None),
        P("dp"),
        P(("dp", "tensor"), None),
    )
    return jax.shard_map(
        on_device,
        mesh=mesh,
        in_specs=placed,
        out_specs=(
            P(("dp", "tensor"), None),
            P(("dp", "tensor"), None),
            P("dp", "tensor"),
            P(),
            P("dp", "tensor"),
            P("dp", "tensor"),
            P(),
            P("tensor", "dp"),
            P(),
            P(),
            P(),
            P("dp", "tensor"),
            P(),
            P("tensor", "dp"),
            P(),
            P(),
            P(),
        ),
        check_vma=False,
    )
```

```python
import jax
import jax.numpy as jnp
from jax import lax
from jax.experimental import pallas as pl
from jax.experimental.pallas import tpu as pltpu
from jax.sharding import PartitionSpec as P

HEAD_DIM = 64


norm_epsilon = 1e-12
masked_score = -1e30


def normalize(matrix, gain, shift):
    center = matrix - jnp.mean(matrix, axis=-1, keepdims=True)
    spread = jnp.mean(center * center, axis=-1, keepdims=True)
    return center * lax.rsqrt(spread + norm_epsilon) * gain + shift


def block_scores(query_block, key_seq, segment_row, valid_count, first_row):
    block_rows = query_block.shape[0]
    length = key_seq.shape[0]
    scores = (
        jnp.einsum("qhd,khd->hqk", query_block, key_seq, preferred_element_type=jnp.float32) * 0.125
    )
    positions = jnp.arange(length, dtype=jnp.int32)
    query_pos = first_row + jnp.arange(block_rows, dtype=jnp.int32)
    query_seg = lax.dynamic_slice_in_dim(segment_row, first_row, block_rows)
    allowed = (query_seg[:, None] == segment_row[None, :]) & (
        (positions[None, :] < valid_count) | (query_pos[:, None] == positions[None, :])
    )
    return jnp.where(allowed[None], scores, masked_score)


def attend_sequence(pieces):
    query_seq, key_seq, value_seq, segment_row, valid_count = pieces
    length = query_seq.shape[0]
    block_rows = min(512, length)

    def one_block(block_index):
        first_row = block_index * block_rows
        query_block = lax.dynamic_slice_in_dim(query_seq, first_row, block_rows)
        masked = block_scores(query_block, key_seq, segment_row, valid_count, first_row)
        largest = jnp.max(masked, axis=-1, keepdims=True)
        totals = jnp.sum(jnp.exp(masked - largest), axis=-1, keepdims=True)
        log_total = largest + jnp.log(totals)
        probs_low = jnp.exp(masked - log_total).astype(jnp.bfloat16)
        context = jnp.einsum(
            "hqk,khd->qhd", probs_low, value_seq, preferred_element_type=jnp.float32
        )
        return (context.astype(jnp.bfloat16), log_total[..., 0])

    contexts, log_totals = lax.map(one_block, jnp.arange(length // block_rows, dtype=jnp.int32))
    return (contexts.reshape(query_seq.shape), log_totals)


def attend_backward(pieces):
    query_seq, key_seq, value_seq, segment_row, valid_count, grad_seq, log_totals = pieces
    length = query_seq.shape[0]
    block_rows = min(512, length)

    def one_block(running, inputs):
        key_grad, value_grad = running
        block_index, log_total = inputs
        first_row = block_index * block_rows
        query_block = lax.dynamic_slice_in_dim(query_seq, first_row, block_rows)
        grad_block = lax.dynamic_slice_in_dim(grad_seq, first_row, block_rows)
        masked = block_scores(query_block, key_seq, segment_row, valid_count, first_row)
        probs = jnp.exp(masked - log_total[..., None])
        probs_low = probs.astype(jnp.bfloat16)
        value_grad = value_grad + jnp.einsum(
            "hqk,qhd->khd", probs_low, grad_block, preferred_element_type=jnp.float32
        )
        d_probs = jnp.einsum(
            "qhd,khd->hqk", grad_block, value_seq, preferred_element_type=jnp.float32
        )
        row_inner = jnp.sum(probs * d_probs, axis=-1, keepdims=True)
        d_scores = (probs * (d_probs - row_inner)).astype(jnp.bfloat16)
        query_grad = (
            jnp.einsum("hqk,khd->qhd", d_scores, key_seq, preferred_element_type=jnp.float32)
            * 0.125
        )
        key_grad = (
            key_grad
            + jnp.einsum("hqk,qhd->khd", d_scores, query_block, preferred_element_type=jnp.float32)
            * 0.125
        )
        return ((key_grad, value_grad), query_grad.astype(jnp.bfloat16))

    empty = jnp.zeros(key_seq.shape, jnp.float32)
    block_ids = jnp.arange(length // block_rows, dtype=jnp.int32)
    (key_grad, value_grad), query_grads = lax.scan(
        one_block, (empty, empty), (block_ids, log_totals)
    )
    return (
        query_grads.reshape(query_seq.shape),
        key_grad.astype(jnp.bfloat16),
        value_grad.astype(jnp.bfloat16),
    )


def slope_and_gelu(inner):
    rise = 0.5 * (1.0 + lax.erf(inner * 0.7071067811865476))
    density = jnp.exp(-0.5 * inner * inner) * 0.3989422804014327
    return inner * rise, rise + inner * density


def norm_backward(matrix, gain, grad):
    center = matrix - jnp.mean(matrix, axis=-1, keepdims=True)
    spread = jnp.mean(center * center, axis=-1, keepdims=True)
    scale = lax.rsqrt(spread + norm_epsilon)
    normed = center * scale
    d_normed = grad * gain
    pulled = scale * (
        d_normed
        - jnp.mean(d_normed, axis=-1, keepdims=True)
        - normed * jnp.mean(d_normed * normed, axis=-1, keepdims=True)
    )
    return pulled, jnp.sum(grad * normed, axis=0), jnp.sum(grad, axis=0)


def halves_in_order(mine, other, shard_index):
    first = shard_index == 0
    return jnp.where(first, mine, other), jnp.where(first, other, mine)


def mix(left, right, dims):
    return lax.dot_general(left, right, (dims, ((), ())), preferred_element_type=jnp.float32)


SWAP = [(0, 1), (1, 0)]


def flip(array, bit):
    if bit == "x":
        return lax.ppermute(array, "tensor", SWAP)
    step = {"core": 1, "y": 2}[bit]
    return lax.ppermute(array, "dp", [(i, i ^ step) for i in range(16)])


def turn(array, shift):
    return lax.ppermute(array, "dp", [(i, (i + 4 * shift) % 16) for i in range(16)])


def whereabouts():
    index = lax.axis_index("dp")
    return dict(z=index // 4, y=(index // 2) % 2, core=index % 2, x=lax.axis_index("tensor"))


def around_z(block):
    return jnp.stack([block] + [turn(block, shift) for shift in (1, 2, 3)])


def spread(block, route):
    near = around_z(block)
    if route == "y":
        plane = {(0, 0): near, (0, 1): flip(near, "y")}
        if_far = []
    else:
        over_x, over_y = flip(near, "x"), flip(near, "y")
        far = flip(over_x, "y") if route == "xy" else flip(over_y, "x")
        plane = {(0, 0): near, (1, 0): over_x, (0, 1): over_y, (1, 1): far}
    pieces = {(0,) + at: piece for at, piece in plane.items()}
    pieces.update({(1,) + at: flip(piece, "core") for at, piece in plane.items()})
    return pieces


def assemble(pieces, place, parts):
    keys = sorted(pieces)
    many_x = 2 if any(key[1] for key in keys) else 1
    rows = pieces[keys[0]].shape[1]
    outs = [
        jax.ShapeDtypeStruct((4, 2, 2, rows, many_x * cols), jnp.bfloat16) for _, cols in parts
    ]

    def body(spot, *refs):
        sources, targets = refs[: len(keys)], refs[len(keys) :]
        for number, (core_off, x_off, y_off) in enumerate(keys):
            core = (spot[2] + core_off) % 2
            y = (spot[1] + y_off) % 2
            x = (spot[3] + x_off) % 2 if many_x == 2 else 0
            for target, (start, cols) in zip(targets, parts):
                column = pl.multiple_of(x * cols, 128) if many_x == 2 else 0
                target[0, y, core, :, pl.ds(column, cols)] = sources[number][
                    0, :, start : start + cols
                ]

    spot = jnp.stack([place[name] for name in ("z", "y", "core", "x")]).astype(jnp.int32)
    piece_spec = pl.BlockSpec((1,) + pieces[keys[0]].shape[1:], lambda i, spot: (i, 0, 0))
    results = pl.pallas_call(
        body,
        out_shape=outs,
        grid_spec=pltpu.PrefetchScalarGridSpec(
            num_scalar_prefetch=1,
            grid=(4,),
            in_specs=[piece_spec] * len(keys),
            out_specs=[
                pl.BlockSpec(
                    (1,) + out.shape[1:], lambda i, spot: ((spot[0] + 4 - i) % 4, 0, 0, 0, 0)
                )
                for out in outs
            ],
        ),
        name="assemble",
    )(spot, *[pieces[key] for key in keys])
    return [result.reshape(16 * rows, result.shape[-1]) for result in results]


def reduce_pieces(grad, place, route, cols):
    low = jnp.bfloat16
    blocks = grad.reshape(4, 2, 2, grad.shape[0] // 16, grad.shape[1])

    def piece(core_off, x_off, y_off):
        core = (place["core"] + core_off) % 2
        y = (place["y"] + y_off) % 2
        x = (place["x"] + x_off) % 2 if grad.shape[1] > cols else 0
        cut = lax.dynamic_slice(
            blocks,
            (0, y, core, 0, x * cols),
            (4, 1, 1, blocks.shape[3], cols),
        )
        return cut.reshape(4, blocks.shape[3], cols)

    def on_chip(x_off, y_off):
        far = flip(piece(1, x_off, y_off).astype(low), "core")
        return piece(0, x_off, y_off).astype(jnp.float32) + far.astype(jnp.float32)

    def joined(first, *others):
        total = first.astype(jnp.float32)
        for other in others:
            total = total + other.astype(jnp.float32)
        return total

    if route == "y":
        total = joined(on_chip(0, 0), flip(on_chip(0, 1).astype(low), "y"))
    elif route == "xy":
        far = flip(on_chip(1, 1).astype(low), "x")
        over_x = flip(on_chip(1, 0).astype(low), "x")
        over_y = flip(joined(on_chip(0, 1), far).astype(low), "y")
        total = joined(on_chip(0, 0), over_x, over_y)
    else:
        far = flip(on_chip(1, 1).astype(low), "y")
        over_y = flip(on_chip(0, 1).astype(low), "y")
        over_x = flip(joined(on_chip(1, 0), far).astype(low), "x")
        total = joined(on_chip(0, 0), over_x, over_y)
    total_low = total.astype(low)

    def for_z(shift):
        return lax.dynamic_index_in_dim(total_low, (place["z"] + shift) % 4, 0, keepdims=False)

    own = lax.dynamic_index_in_dim(total, place["z"], 0, keepdims=False)
    return joined(own, *[turn(for_z(shift), shift) for shift in (1, 2, 3)])


def sum_everywhere(vector):
    for step in (1, 2, 4, 8):
        vector = vector + lax.ppermute(vector, "dp", [(i, i ^ step) for i in range(16)])
    return vector + lax.ppermute(vector, "tensor", SWAP)


def on_device(
    tokens,
    query_weight,
    query_bias,
    key_weight,
    value_weight,
    value_bias,
    output_weight,
    output_bias,
    first_gain,
    first_shift,
    inner_weight,
    inner_bias,
    outer_weight,
    outer_bias,
    second_gain,
    second_shift,
    segments,
    valid_length,
    cotangent,
):
    low = jnp.bfloat16
    whole = ("tensor", "dp")
    by_links = lax.axis_size("dp") == 16
    place = whereabouts()
    own_rows, width = tokens.shape
    head_cols = query_weight.shape[1]
    hidden_cols = inner_weight.shape[1]
    local_heads = head_cols // HEAD_DIM
    shard_index = lax.axis_index("tensor")
    own_start = shard_index * own_rows
    other_start = (1 - shard_index) * own_rows

    other_tokens = lax.ppermute(tokens, "tensor", SWAP)
    packed_qkv = jnp.concatenate([query_weight, key_weight, value_weight], axis=1)
    packed_in = jnp.concatenate([output_weight.T, inner_weight], axis=1)
    packed_out = outer_weight.T
    if by_links:
        (full_qkv,) = assemble(spread(packed_qkv, "y"), place, [(0, 3 * head_cols)])
        full_output, full_inner = assemble(
            spread(packed_in, "yx"), place, [(0, head_cols), (head_cols, hidden_cols)]
        )
        (full_outer,) = assemble(spread(packed_out, "xy"), place, [(0, hidden_cols)])
    else:
        full_qkv = lax.all_gather(packed_qkv, "dp", axis=0, tiled=True)
        gathered = lax.all_gather(packed_in, whole, axis=0, tiled=True)
        gathered = gathered.reshape(2, width, head_cols + hidden_cols)
        full_output = jnp.concatenate([gathered[0, :, :head_cols], gathered[1, :, :head_cols]], 1)
        full_inner = jnp.concatenate([gathered[0, :, head_cols:], gathered[1, :, head_cols:]], 1)
        gathered = lax.all_gather(packed_out, whole, axis=0, tiled=True)
        gathered = gathered.reshape(2, width, hidden_cols)
        full_outer = jnp.concatenate([gathered[0], gathered[1]], 1)

    group_rows = jnp.concatenate(halves_in_order(tokens, other_tokens, shard_index), axis=0)
    bias_query = lax.dynamic_slice_in_dim(query_bias, shard_index * head_cols, head_cols)
    bias_value = lax.dynamic_slice_in_dim(value_bias, shard_index * head_cols, head_cols)
    bias_qkv = jnp.concatenate([bias_query, jnp.zeros_like(bias_query), bias_value])
    seq_count, seq_length = segments.shape
    four_shape = (seq_count, seq_length, local_heads, HEAD_DIM)
    qkv = (mix(group_rows, full_qkv, ((1,), (0,))) + bias_qkv).astype(low)
    queries = qkv[:, :head_cols].reshape(four_shape)
    keys_all = qkv[:, head_cols : 2 * head_cols].reshape(four_shape)
    values_all = qkv[:, 2 * head_cols :].reshape(four_shape)
    contexts, log_totals = lax.map(
        attend_sequence, (queries, keys_all, values_all, segments, valid_length)
    )
    context = contexts.reshape(seq_count * seq_length, head_cols)
    own_context = lax.dynamic_slice_in_dim(context, own_start, own_rows)
    far_context = lax.ppermute(
        lax.dynamic_slice_in_dim(context, other_start, own_rows), "tensor", SWAP
    )
    context_halves = halves_in_order(own_context, far_context, shard_index)
    own_rows_context = jnp.concatenate(context_halves, axis=1)
    attended = mix(own_rows_context, full_output, ((1,), (1,)))
    first_sum = tokens.astype(jnp.float32) + attended + output_bias
    hidden = normalize(first_sum, first_gain, first_shift)
    hidden_low = hidden.astype(low)
    inner = mix(hidden_low, full_inner, ((1,), (0,))) + inner_bias
    value, slope = slope_and_gelu(inner)
    activated = value.astype(low)
    second_sum = hidden + mix(activated, full_outer, ((1,), (1,))) + outer_bias
    layer_output = normalize(second_sum, second_gain, second_shift).astype(low)
    d_second, second_gain_grad, second_shift_grad = norm_backward(
        second_sum, second_gain, cotangent.astype(jnp.float32)
    )
    outer_bias_grad = jnp.sum(d_second, axis=0)
    d_outer = d_second.astype(low)
    outer_weight_grad = mix(d_outer, activated, ((0,), (0,))).astype(low)
    d_activated = mix(d_outer, full_outer, ((1,), (0,)))
    d_inner = (d_activated * slope).astype(low)
    inner_weight_grad = mix(hidden_low, d_inner, ((0,), (0,))).astype(low)
    inner_bias_grad = jnp.sum(d_inner, axis=0, dtype=jnp.float32)
    d_hidden = d_second + mix(d_inner, full_inner, ((1,), (1,)))
    d_first, first_gain_grad, first_shift_grad = norm_backward(first_sum, first_gain, d_hidden)
    output_bias_grad = jnp.sum(d_first, axis=0)
    d_attended = d_first.astype(low)
    output_weight_grad = mix(d_attended, own_rows_context, ((0,), (0,))).astype(low)
    d_own_context = mix(d_attended, full_output, ((1,), (0,))).astype(low)
    d_context_halves = (d_own_context[:, :head_cols], d_own_context[:, head_cols:])
    first = shard_index == 0
    own_d_context = jnp.where(first, d_context_halves[0], d_context_halves[1])
    far_d_context = lax.ppermute(
        jnp.where(first, d_context_halves[1], d_context_halves[0]), "tensor", SWAP
    )
    d_context = jnp.concatenate(
        halves_in_order(own_d_context, far_d_context, shard_index), axis=0
    )
    d_queries, d_keys, d_values = lax.map(
        attend_backward,
        (
            queries,
            keys_all,
            values_all,
            segments,
            valid_length,
            d_context.reshape(four_shape),
            log_totals,
        ),
    )
    flat = (seq_count * seq_length, head_cols)
    d_qkv = jnp.concatenate(
        [d_queries.reshape(flat), d_keys.reshape(flat), d_values.reshape(flat)], axis=1
    )
    qkv_weight_grad = mix(group_rows, d_qkv, ((0,), (0,))).astype(low)
    partial_input = mix(d_qkv, full_qkv, ((1,), (1,)))
    far_input = lax.ppermute(
        lax.dynamic_slice_in_dim(partial_input, other_start, own_rows).astype(low), "tensor", SWAP
    )
    input_gradient = (
        d_first
        + lax.dynamic_slice_in_dim(partial_input, own_start, own_rows)
        + far_input.astype(jnp.float32)
    )

    def scatter(grad, axes, route, cols):
        if by_links:
            return reduce_pieces(grad, place, route, cols)
        if grad.shape[1] > cols:
            grad = jnp.concatenate([grad[:, :cols], grad[:, cols:]], axis=0)
        return lax.psum_scatter(grad, axes, scatter_dimension=0, tiled=True).astype(jnp.float32)

    outer_shard = scatter(outer_weight_grad, whole, "xy", hidden_cols).T
    inner_shard = scatter(inner_weight_grad, whole, "yx", hidden_cols)
    output_shard = scatter(output_weight_grad, whole, "yx", head_cols).T
    qkv_shard = scatter(qkv_weight_grad, ("dp",), "y", 3 * head_cols)
    bias_local = jnp.sum(d_qkv, axis=0, dtype=jnp.float32)
    spread_out = lax.dynamic_update_slice(
        jnp.zeros((2, width), jnp.float32),
        jnp.stack([bias_local[:head_cols], bias_local[2 * head_cols :]]),
        (0, shard_index * head_cols),
    )
    early = [
        output_bias_grad,
        first_gain_grad,
        first_shift_grad,
        outer_bias_grad,
        second_gain_grad,
        second_shift_grad,
        inner_bias_grad,
    ]
    if by_links:
        early_sum = sum_everywhere(jnp.concatenate(early).reshape(-1, 128)).reshape(-1)
        late_sum = sum_everywhere(spread_out.reshape(-1, 128)).reshape(-1)
    else:
        late_sum, early_sum = lax.psum(
            (spread_out.reshape(-1), jnp.concatenate(early)), ("dp", "tensor")
        )
    rows = [late_sum[:width], late_sum[width:]] + [
        early_sum[at * width : (at + 1) * width] for at in range(6)
    ]
    summed_inner = early_sum[6 * width :]
    return (
        layer_output,
        input_gradient,
        qkv_shard[:, :head_cols],
        rows[0],
        qkv_shard[:, head_cols : 2 * head_cols],
        qkv_shard[:, 2 * head_cols :],
        rows[1],
        output_shard,
        rows[2],
        rows[3],
        rows[4],
        inner_shard,
        summed_inner,
        outer_shard,
        rows[5],
        rows[6],
        rows[7],
    )


def solution(mesh):
    placed = (
        P(("dp", "tensor"), None),
        P("dp", "tensor"),
        P(),
        P("dp", "tensor"),
        P("dp", "tensor"),
        P(),
        P("tensor", "dp"),
        P(),
        P(),
        P(),
        P("dp", "tensor"),
        P(),
        P("tensor", "dp"),
        P(),
        P(),
        P(),
        P("dp", None),
        P("dp"),
        P(("dp", "tensor"), None),
    )
    return jax.shard_map(
        on_device,
        mesh=mesh,
        in_specs=placed,
        out_specs=(
            P(("dp", "tensor"), None),
            P(("dp", "tensor"), None),
            P("dp", "tensor"),
            P(),
            P("dp", "tensor"),
            P("dp", "tensor"),
            P(),
            P("tensor", "dp"),
            P(),
            P(),
            P(),
            P("dp", "tensor"),
            P(),
            P("tensor", "dp"),
            P(),
            P(),
            P(),
        ),
        check_vma=False,
    )
```

```python
import jax
import jax.numpy as jnp
from jax import lax
from jax.experimental import pallas as pl
from jax.experimental.pallas import tpu as pltpu
from jax.sharding import PartitionSpec as P

HEAD_DIM = 64


norm_epsilon = 1e-12
masked_score = -1e30


def normalize(matrix, gain, shift):
    center = matrix - jnp.mean(matrix, axis=-1, keepdims=True)
    spread = jnp.mean(center * center, axis=-1, keepdims=True)
    return center * lax.rsqrt(spread + norm_epsilon) * gain + shift


LOG2_E = 1.4426950408889634
QUERY_ROWS = 256


def two_heads(rows):
    lane = lax.broadcasted_iota(jnp.int32, rows.shape, 1)
    zero = jnp.zeros_like(rows)
    return jnp.concatenate(
        [jnp.where(lane < HEAD_DIM, rows, zero), jnp.where(lane < HEAD_DIM, zero, rows)], axis=0
    )


def pick_heads(columns):
    count = columns.shape[1] // 2
    row = lax.broadcasted_iota(jnp.int32, (columns.shape[0], count), 0)
    return jnp.where(row < HEAD_DIM, columns[:, :count], columns[:, count:]).T


def masked_scores(keys, queries_two, key_marks, query_marks, first_row):
    scores = lax.dot_general(
        keys, queries_two, (((1,), (1,)), ((), ())), preferred_element_type=jnp.float32
    ) * (0.125 * LOG2_E)
    count = queries_two.shape[0] // 2
    length = keys.shape[0]
    query_two = jnp.concatenate([query_marks, query_marks], axis=1)
    marks = jnp.concatenate([key_marks] * (2 * count // key_marks.shape[1]), axis=1)
    allowed = marks == query_two
    pieces = []
    for start in range(0, length, count):
        part = allowed[start : start + count]
        if start == first_row:
            row = lax.broadcasted_iota(jnp.int32, (count, 2 * count), 0)
            column = lax.broadcasted_iota(jnp.int32, (count, 2 * count), 1)
            part = part | (row == jnp.where(column < count, column, column - count))
        pieces.append(jnp.where(part, scores[start : start + count], masked_score))
    return jnp.concatenate(pieces, axis=0)


def forward_body(query_ref, key_ref, value_ref, key_marks_ref, query_marks_ref, out_ref, lse_ref):
    length = key_ref.shape[0]
    keys = key_ref[...]
    values_t = value_ref[...].T
    for first_row in range(0, length, QUERY_ROWS):
        rows = pl.ds(first_row, QUERY_ROWS)
        scores = masked_scores(
            keys,
            two_heads(query_ref[rows, :]),
            key_marks_ref[...],
            query_marks_ref[0, :, rows],
            first_row,
        )
        largest = jnp.max(scores, axis=0, keepdims=True)
        powers = jnp.exp2(scores - largest)
        totals = jnp.sum(powers, axis=0, keepdims=True)
        product = lax.dot_general(
            values_t,
            powers.astype(jnp.bfloat16),
            (((1,), (0,)), ((), ())),
            preferred_element_type=jnp.float32,
        )
        out_ref[rows, :] = pick_heads(product * (1.0 / totals)).astype(jnp.bfloat16)
        lse_ref[0, 0, :, pl.ds(2 * first_row, 2 * QUERY_ROWS)] = largest + jnp.log2(totals)


def backward_body(
    query_ref, key_ref, value_ref, grad_ref, key_marks_ref, query_marks_ref, lse_ref, out_ref,
    key_sum, value_sum,
):
    length = key_ref.shape[0]
    width = out_ref.shape[1] // 3
    low = jnp.bfloat16
    keys = key_ref[...]
    values = value_ref[...]
    keys_t = keys.T
    column = pl.multiple_of(pl.program_id(1) * 2 * HEAD_DIM, 2 * HEAD_DIM)
    for first_row in range(0, length, QUERY_ROWS):
        rows = pl.ds(first_row, QUERY_ROWS)
        queries_two = two_heads(query_ref[rows, :])
        grads_two = two_heads(grad_ref[rows, :])
        scores = masked_scores(
            keys, queries_two, key_marks_ref[...], query_marks_ref[0, :, rows], first_row
        )
        probs = jnp.exp2(scores - lse_ref[0, 0, :, pl.ds(2 * first_row, 2 * QUERY_ROWS)])
        d_probs = lax.dot_general(
            values, grads_two, (((1,), (1,)), ((), ())), preferred_element_type=jnp.float32
        )
        inner = jnp.sum(probs * d_probs, axis=0, keepdims=True)
        d_scores = (probs * (d_probs - inner)).astype(low)
        value_part = lax.dot_general(
            probs.astype(low), grads_two, (((1,), (0,)), ((), ())),
            preferred_element_type=jnp.float32,
        )
        key_part = lax.dot_general(
            d_scores, queries_two, (((1,), (0,)), ((), ())), preferred_element_type=jnp.float32
        )
        if first_row == 0:
            value_sum[...] = value_part
            key_sum[...] = key_part
        else:
            value_sum[...] += value_part
            key_sum[...] += key_part
        query_part = lax.dot_general(
            keys_t, d_scores, (((1,), (0,)), ((), ())), preferred_element_type=jnp.float32
        )
        out_ref[rows, pl.ds(column, 2 * HEAD_DIM)] = (pick_heads(query_part) * 0.125).astype(low)
    out_ref[:, pl.ds(column + width, 2 * HEAD_DIM)] = (key_sum[...] * 0.125).astype(low)
    out_ref[:, pl.ds(column + 2 * width, 2 * HEAD_DIM)] = value_sum[...].astype(low)


def attention_marks(segments, valid_length):
    seq_count, length = segments.shape
    positions = jnp.arange(length, dtype=jnp.int32)
    key_marks = jnp.where(positions[None, :] < valid_length[:, None], segments, -1)
    key_marks = jnp.broadcast_to(key_marks.reshape(-1, 1), (seq_count * length, 128))
    return key_marks, segments.reshape(seq_count, 1, length)


def pair_specs(length, pairs, blocks):
    return [
        pl.BlockSpec((length, 2 * HEAD_DIM), lambda s, p, at=at: (s, at * pairs + p))
        for at in blocks
    ]


def attend_forward(qkv, key_marks, query_marks):
    seq_count, _, length = query_marks.shape
    pairs = qkv.shape[1] // (6 * HEAD_DIM)
    return pl.pallas_call(
        forward_body,
        out_shape=(
            jax.ShapeDtypeStruct((qkv.shape[0], qkv.shape[1] // 3), jnp.bfloat16),
            jax.ShapeDtypeStruct((seq_count, pairs, 1, 2 * length), jnp.float32),
        ),
        grid=(seq_count, pairs),
        in_specs=pair_specs(length, pairs, (0, 1, 2))
        + [
            pl.BlockSpec((length, 128), lambda s, p: (s, 0)),
            pl.BlockSpec((1, 1, length), lambda s, p: (s, 0, 0)),
        ],
        out_specs=(
            pl.BlockSpec((length, 2 * HEAD_DIM), lambda s, p: (s, p)),
            pl.BlockSpec((1, 1, 1, 2 * length), lambda s, p: (s, p, 0, 0)),
        ),
        name="attend_forward",
    )(qkv, qkv, qkv, key_marks, query_marks)


def attend_backward(qkv, grad, key_marks, query_marks, lse):
    seq_count, _, length = query_marks.shape
    pairs = qkv.shape[1] // (6 * HEAD_DIM)
    return pl.pallas_call(
        backward_body,
        out_shape=jax.ShapeDtypeStruct(qkv.shape, jnp.bfloat16),
        grid=(seq_count, pairs),
        in_specs=pair_specs(length, pairs, (0, 1, 2, 0))
        + [
            pl.BlockSpec((length, 128), lambda s, p: (s, 0)),
            pl.BlockSpec((1, 1, length), lambda s, p: (s, 0, 0)),
            pl.BlockSpec((1, 1, 1, 2 * length), lambda s, p: (s, p, 0, 0)),
        ],
        out_specs=pl.BlockSpec((length, qkv.shape[1]), lambda s, p: (s, 0)),
        scratch_shapes=[pltpu.VMEM((length, 2 * HEAD_DIM), jnp.float32)] * 2,
        name="attend_backward",
    )(qkv, qkv, qkv, grad, key_marks, query_marks, lse)


def slope_and_gelu(inner):
    rise = 0.5 * (1.0 + lax.erf(inner * 0.7071067811865476))
    density = jnp.exp(-0.5 * inner * inner) * 0.3989422804014327
    return inner * rise, rise + inner * density


def norm_backward(matrix, gain, grad):
    center = matrix - jnp.mean(matrix, axis=-1, keepdims=True)
    spread = jnp.mean(center * center, axis=-1, keepdims=True)
    scale = lax.rsqrt(spread + norm_epsilon)
    normed = center * scale
    d_normed = grad * gain
    pulled = scale * (
        d_normed
        - jnp.mean(d_normed, axis=-1, keepdims=True)
        - normed * jnp.mean(d_normed * normed, axis=-1, keepdims=True)
    )
    return pulled, jnp.sum(grad * normed, axis=0), jnp.sum(grad, axis=0)


def halves_in_order(mine, other, shard_index):
    first = shard_index == 0
    return jnp.where(first, mine, other), jnp.where(first, other, mine)


def mix(left, right, dims):
    return lax.dot_general(left, right, (dims, ((), ())), preferred_element_type=jnp.float32)


SWAP = [(0, 1), (1, 0)]


def flip(array, bit):
    if bit == "x":
        return lax.ppermute(array, "tensor", SWAP)
    step = {"core": 1, "y": 2}[bit]
    return lax.ppermute(array, "dp", [(i, i ^ step) for i in range(16)])


def turn(array, shift):
    return lax.ppermute(array, "dp", [(i, (i + 4 * shift) % 16) for i in range(16)])


def whereabouts():
    index = lax.axis_index("dp")
    return dict(z=index // 4, y=(index // 2) % 2, core=index % 2, x=lax.axis_index("tensor"))


def around_z(block):
    return jnp.stack([block] + [turn(block, shift) for shift in (1, 2, 3)])


def spread(block, route):
    near = around_z(block)
    if route == "y":
        plane = {(0, 0): near, (0, 1): flip(near, "y")}
        if_far = []
    else:
        over_x, over_y = flip(near, "x"), flip(near, "y")
        far = flip(over_x, "y") if route == "xy" else flip(over_y, "x")
        plane = {(0, 0): near, (1, 0): over_x, (0, 1): over_y, (1, 1): far}
    pieces = {(0,) + at: piece for at, piece in plane.items()}
    pieces.update({(1,) + at: flip(piece, "core") for at, piece in plane.items()})
    return pieces


def assemble(pieces, place, parts):
    keys = sorted(pieces)
    many_x = 2 if any(key[1] for key in keys) else 1
    rows = pieces[keys[0]].shape[1]
    outs = [
        jax.ShapeDtypeStruct((4, 2, 2, rows, many_x * cols), jnp.bfloat16) for _, cols in parts
    ]

    def body(spot, *refs):
        sources, targets = refs[: len(keys)], refs[len(keys) :]
        for number, (core_off, x_off, y_off) in enumerate(keys):
            core = (spot[2] + core_off) % 2
            y = (spot[1] + y_off) % 2
            x = (spot[3] + x_off) % 2 if many_x == 2 else 0
            for target, (start, cols) in zip(targets, parts):
                column = pl.multiple_of(x * cols, 128) if many_x == 2 else 0
                target[0, y, core, :, pl.ds(column, cols)] = sources[number][
                    0, :, start : start + cols
                ]

    spot = jnp.stack([place[name] for name in ("z", "y", "core", "x")]).astype(jnp.int32)
    piece_spec = pl.BlockSpec((1,) + pieces[keys[0]].shape[1:], lambda i, spot: (i, 0, 0))
    results = pl.pallas_call(
        body,
        out_shape=outs,
        grid_spec=pltpu.PrefetchScalarGridSpec(
            num_scalar_prefetch=1,
            grid=(4,),
            in_specs=[piece_spec] * len(keys),
            out_specs=[
                pl.BlockSpec(
                    (1,) + out.shape[1:], lambda i, spot: ((spot[0] + 4 - i) % 4, 0, 0, 0, 0)
                )
                for out in outs
            ],
        ),
        name="assemble",
    )(spot, *[pieces[key] for key in keys])
    return [result.reshape(16 * rows, result.shape[-1]) for result in results]


def reduce_pieces(grad, place, route, cols):
    low = jnp.bfloat16
    blocks = grad.reshape(4, 2, 2, grad.shape[0] // 16, grad.shape[1])

    def piece(core_off, x_off, y_off):
        core = (place["core"] + core_off) % 2
        y = (place["y"] + y_off) % 2
        x = (place["x"] + x_off) % 2 if grad.shape[1] > cols else 0
        cut = lax.dynamic_slice(
            blocks,
            (0, y, core, 0, x * cols),
            (4, 1, 1, blocks.shape[3], cols),
        )
        return cut.reshape(4, blocks.shape[3], cols)

    def on_chip(x_off, y_off):
        far = flip(piece(1, x_off, y_off).astype(low), "core")
        return piece(0, x_off, y_off).astype(jnp.float32) + far.astype(jnp.float32)

    def joined(first, *others):
        total = first.astype(jnp.float32)
        for other in others:
            total = total + other.astype(jnp.float32)
        return total

    if route == "y":
        total = joined(on_chip(0, 0), flip(on_chip(0, 1).astype(low), "y"))
    elif route == "xy":
        far = flip(on_chip(1, 1).astype(low), "x")
        over_x = flip(on_chip(1, 0).astype(low), "x")
        over_y = flip(joined(on_chip(0, 1), far).astype(low), "y")
        total = joined(on_chip(0, 0), over_x, over_y)
    else:
        far = flip(on_chip(1, 1).astype(low), "y")
        over_y = flip(on_chip(0, 1).astype(low), "y")
        over_x = flip(joined(on_chip(1, 0), far).astype(low), "x")
        total = joined(on_chip(0, 0), over_x, over_y)
    total_low = total.astype(low)

    def for_z(shift):
        return lax.dynamic_index_in_dim(total_low, (place["z"] + shift) % 4, 0, keepdims=False)

    own = lax.dynamic_index_in_dim(total, place["z"], 0, keepdims=False)
    return joined(own, *[turn(for_z(shift), shift) for shift in (1, 2, 3)])


def sum_everywhere(vector):
    for step in (1, 2, 4, 8):
        vector = vector + lax.ppermute(vector, "dp", [(i, i ^ step) for i in range(16)])
    return vector + lax.ppermute(vector, "tensor", SWAP)


def on_device(
    tokens,
    query_weight,
    query_bias,
    key_weight,
    value_weight,
    value_bias,
    output_weight,
    output_bias,
    first_gain,
    first_shift,
    inner_weight,
    inner_bias,
    outer_weight,
    outer_bias,
    second_gain,
    second_shift,
    segments,
    valid_length,
    cotangent,
):
    low = jnp.bfloat16
    whole = ("tensor", "dp")
    by_links = lax.axis_size("dp") == 16
    place = whereabouts()
    own_rows, width = tokens.shape
    head_cols = query_weight.shape[1]
    hidden_cols = inner_weight.shape[1]
    shard_index = lax.axis_index("tensor")
    own_start = shard_index * own_rows
    other_start = (1 - shard_index) * own_rows

    other_tokens = lax.ppermute(tokens, "tensor", SWAP)
    packed_qkv = jnp.concatenate([query_weight, key_weight, value_weight], axis=1)
    packed_in = jnp.concatenate([output_weight.T, inner_weight], axis=1)
    packed_out = outer_weight.T
    if by_links:
        (full_qkv,) = assemble(spread(packed_qkv, "y"), place, [(0, 3 * head_cols)])
        full_output, full_inner = assemble(
            spread(packed_in, "yx"), place, [(0, head_cols), (head_cols, hidden_cols)]
        )
        (full_outer,) = assemble(spread(packed_out, "xy"), place, [(0, hidden_cols)])
    else:
        full_qkv = lax.all_gather(packed_qkv, "dp", axis=0, tiled=True)
        gathered = lax.all_gather(packed_in, whole, axis=0, tiled=True)
        gathered = gathered.reshape(2, width, head_cols + hidden_cols)
        full_output = jnp.concatenate([gathered[0, :, :head_cols], gathered[1, :, :head_cols]], 1)
        full_inner = jnp.concatenate([gathered[0, :, head_cols:], gathered[1, :, head_cols:]], 1)
        gathered = lax.all_gather(packed_out, whole, axis=0, tiled=True)
        gathered = gathered.reshape(2, width, hidden_cols)
        full_outer = jnp.concatenate([gathered[0], gathered[1]], 1)

    group_rows = jnp.concatenate(halves_in_order(tokens, other_tokens, shard_index), axis=0)
    bias_query = lax.dynamic_slice_in_dim(query_bias, shard_index * head_cols, head_cols)
    bias_value = lax.dynamic_slice_in_dim(value_bias, shard_index * head_cols, head_cols)
    bias_qkv = jnp.concatenate([bias_query, jnp.zeros_like(bias_query), bias_value])
    qkv = (mix(group_rows, full_qkv, ((1,), (0,))) + bias_qkv).astype(low)
    key_marks, query_marks = attention_marks(segments, valid_length)
    context, log_totals = attend_forward(qkv, key_marks, query_marks)
    own_context = lax.dynamic_slice_in_dim(context, own_start, own_rows)
    far_context = lax.ppermute(
        lax.dynamic_slice_in_dim(context, other_start, own_rows), "tensor", SWAP
    )
    context_halves = halves_in_order(own_context, far_context, shard_index)
    own_rows_context = jnp.concatenate(context_halves, axis=1)
    attended = mix(own_rows_context, full_output, ((1,), (1,)))
    first_sum = tokens.astype(jnp.float32) + attended + output_bias
    hidden = normalize(first_sum, first_gain, first_shift)
    hidden_low = hidden.astype(low)
    inner = mix(hidden_low, full_inner, ((1,), (0,))) + inner_bias
    value, slope = slope_and_gelu(inner)
    activated = value.astype(low)
    second_sum = hidden + mix(activated, full_outer, ((1,), (1,))) + outer_bias
    layer_output = normalize(second_sum, second_gain, second_shift).astype(low)
    d_second, second_gain_grad, second_shift_grad = norm_backward(
        second_sum, second_gain, cotangent.astype(jnp.float32)
    )
    outer_bias_grad = jnp.sum(d_second, axis=0)
    d_outer = d_second.astype(low)
    outer_weight_grad = mix(d_outer, activated, ((0,), (0,))).astype(low)
    d_activated = mix(d_outer, full_outer, ((1,), (0,)))
    d_inner = (d_activated * slope).astype(low)
    inner_weight_grad = mix(hidden_low, d_inner, ((0,), (0,))).astype(low)
    inner_bias_grad = jnp.sum(d_inner, axis=0, dtype=jnp.float32)
    d_hidden = d_second + mix(d_inner, full_inner, ((1,), (1,)))
    d_first, first_gain_grad, first_shift_grad = norm_backward(first_sum, first_gain, d_hidden)
    output_bias_grad = jnp.sum(d_first, axis=0)
    d_attended = d_first.astype(low)
    output_weight_grad = mix(d_attended, own_rows_context, ((0,), (0,))).astype(low)
    d_own_context = mix(d_attended, full_output, ((1,), (0,))).astype(low)
    d_context_halves = (d_own_context[:, :head_cols], d_own_context[:, head_cols:])
    first = shard_index == 0
    own_d_context = jnp.where(first, d_context_halves[0], d_context_halves[1])
    far_d_context = lax.ppermute(
        jnp.where(first, d_context_halves[1], d_context_halves[0]), "tensor", SWAP
    )
    d_context = jnp.concatenate(
        halves_in_order(own_d_context, far_d_context, shard_index), axis=0
    )
    d_qkv = attend_backward(qkv, d_context, key_marks, query_marks, log_totals)
    qkv_weight_grad = mix(group_rows, d_qkv, ((0,), (0,))).astype(low)
    partial_input = mix(d_qkv, full_qkv, ((1,), (1,)))
    far_input = lax.ppermute(
        lax.dynamic_slice_in_dim(partial_input, other_start, own_rows).astype(low), "tensor", SWAP
    )
    input_gradient = (
        d_first
        + lax.dynamic_slice_in_dim(partial_input, own_start, own_rows)
        + far_input.astype(jnp.float32)
    )

    def scatter(grad, axes, route, cols):
        if by_links:
            return reduce_pieces(grad, place, route, cols)
        if grad.shape[1] > cols:
            grad = jnp.concatenate([grad[:, :cols], grad[:, cols:]], axis=0)
        return lax.psum_scatter(grad, axes, scatter_dimension=0, tiled=True).astype(jnp.float32)

    outer_shard = scatter(outer_weight_grad, whole, "xy", hidden_cols).T
    inner_shard = scatter(inner_weight_grad, whole, "yx", hidden_cols)
    output_shard = scatter(output_weight_grad, whole, "yx", head_cols).T
    qkv_shard = scatter(qkv_weight_grad, ("dp",), "y", 3 * head_cols)
    bias_local = jnp.sum(d_qkv, axis=0, dtype=jnp.float32)
    spread_out = lax.dynamic_update_slice(
        jnp.zeros((2, width), jnp.float32),
        jnp.stack([bias_local[:head_cols], bias_local[2 * head_cols :]]),
        (0, shard_index * head_cols),
    )
    early = [
        output_bias_grad,
        first_gain_grad,
        first_shift_grad,
        outer_bias_grad,
        second_gain_grad,
        second_shift_grad,
        inner_bias_grad,
    ]
    if by_links:
        early_sum = sum_everywhere(jnp.concatenate(early).reshape(-1, 128)).reshape(-1)
        late_sum = sum_everywhere(spread_out.reshape(-1, 128)).reshape(-1)
    else:
        late_sum, early_sum = lax.psum(
            (spread_out.reshape(-1), jnp.concatenate(early)), ("dp", "tensor")
        )
    rows = [late_sum[:width], late_sum[width:]] + [
        early_sum[at * width : (at + 1) * width] for at in range(6)
    ]
    summed_inner = early_sum[6 * width :]
    return (
        layer_output,
        input_gradient,
        qkv_shard[:, :head_cols],
        rows[0],
        qkv_shard[:, head_cols : 2 * head_cols],
        qkv_shard[:, 2 * head_cols :],
        rows[1],
        output_shard,
        rows[2],
        rows[3],
        rows[4],
        inner_shard,
        summed_inner,
        outer_shard,
        rows[5],
        rows[6],
        rows[7],
    )


def solution(mesh):
    placed = (
        P(("dp", "tensor"), None),
        P("dp", "tensor"),
        P(),
        P("dp", "tensor"),
        P("dp", "tensor"),
        P(),
        P("tensor", "dp"),
        P(),
        P(),
        P(),
        P("dp", "tensor"),
        P(),
        P("tensor", "dp"),
        P(),
        P(),
        P(),
        P("dp", None),
        P("dp"),
        P(("dp", "tensor"), None),
    )
    return jax.shard_map(
        on_device,
        mesh=mesh,
        in_specs=placed,
        out_specs=(
            P(("dp", "tensor"), None),
            P(("dp", "tensor"), None),
            P("dp", "tensor"),
            P(),
            P("dp", "tensor"),
            P("dp", "tensor"),
            P(),
            P("tensor", "dp"),
            P(),
            P(),
            P(),
            P("dp", "tensor"),
            P(),
            P("tensor", "dp"),
            P(),
            P(),
            P(),
        ),
        check_vma=False,
    )
```

```python
import jax
import jax.numpy as jnp
from jax import lax
from jax.experimental import pallas as pl
from jax.experimental.pallas import tpu as pltpu
from jax.sharding import PartitionSpec as P

HEAD_DIM = 64


norm_epsilon = 1e-12
masked_score = -1e30


def normalize(matrix, gain, shift):
    center = matrix - jnp.mean(matrix, axis=-1, keepdims=True)
    spread = jnp.mean(center * center, axis=-1, keepdims=True)
    return center * lax.rsqrt(spread + norm_epsilon) * gain + shift


LOG2_E = 1.4426950408889634
QUERY_ROWS = 256


def two_heads(rows):
    lane = lax.broadcasted_iota(jnp.int32, rows.shape, 1)
    zero = jnp.zeros_like(rows)
    return jnp.concatenate(
        [jnp.where(lane < HEAD_DIM, rows, zero), jnp.where(lane < HEAD_DIM, zero, rows)], axis=0
    )


def pick_heads(columns):
    count = columns.shape[1] // 2
    row = lax.broadcasted_iota(jnp.int32, (columns.shape[0], count), 0)
    return jnp.where(row < HEAD_DIM, columns[:, :count], columns[:, count:]).T


def masked_scores(keys, queries_two, key_marks, query_marks, first_row):
    scores = lax.dot_general(
        keys, queries_two, (((1,), (1,)), ((), ())), preferred_element_type=jnp.float32
    ) * (0.125 * LOG2_E)
    count = queries_two.shape[0] // 2
    length = keys.shape[0]
    query_two = jnp.concatenate([query_marks, query_marks], axis=1)
    marks = jnp.concatenate([key_marks] * (2 * count // key_marks.shape[1]), axis=1)
    allowed = marks == query_two
    pieces = []
    for start in range(0, length, count):
        part = allowed[start : start + count]
        if start == first_row:
            row = lax.broadcasted_iota(jnp.int32, (count, 2 * count), 0)
            column = lax.broadcasted_iota(jnp.int32, (count, 2 * count), 1)
            part = part | (row == jnp.where(column < count, column, column - count))
        pieces.append(jnp.where(part, scores[start : start + count], masked_score))
    return jnp.concatenate(pieces, axis=0)


def forward_body(
    query_ref, key_ref, value_ref, key_marks_ref, query_marks_ref, own_ref, other_ref, lse_ref
):
    length = key_ref.shape[0]
    keys = key_ref[...]
    values_t = value_ref[...].T
    for first_row in range(0, length, QUERY_ROWS):
        rows = pl.ds(first_row, QUERY_ROWS)
        scores = masked_scores(
            keys,
            two_heads(query_ref[rows, :]),
            key_marks_ref[...],
            query_marks_ref[0, :, rows],
            first_row,
        )
        largest = jnp.max(scores, axis=0, keepdims=True)
        powers = jnp.exp2(scores - largest)
        totals = jnp.sum(powers, axis=0, keepdims=True)
        product = lax.dot_general(
            values_t,
            powers.astype(jnp.bfloat16),
            (((1,), (0,)), ((), ())),
            preferred_element_type=jnp.float32,
        )
        target = own_ref if first_row < length // 2 else other_ref
        target[pl.ds(first_row % (length // 2), QUERY_ROWS), :] = pick_heads(
            product * (1.0 / totals)
        ).astype(jnp.bfloat16)
        lse_ref[0, 0, :, pl.ds(2 * first_row, 2 * QUERY_ROWS)] = largest + jnp.log2(totals)


def backward_body(
    query_ref, key_ref, value_ref, own_ref, far_ref, key_marks_ref, query_marks_ref, lse_ref, out_ref,
    key_sum, value_sum,
):
    length = key_ref.shape[0]
    width = out_ref.shape[1] // 3
    low = jnp.bfloat16
    keys = key_ref[...]
    values = value_ref[...]
    keys_t = keys.T
    column = pl.multiple_of(pl.program_id(1) * 2 * HEAD_DIM, 2 * HEAD_DIM)
    for first_row in range(0, length, QUERY_ROWS):
        rows = pl.ds(first_row, QUERY_ROWS)
        queries_two = two_heads(query_ref[rows, :])
        grad_ref = own_ref if first_row < length // 2 else far_ref
        grads_two = two_heads(grad_ref[pl.ds(first_row % (length // 2), QUERY_ROWS), :])
        scores = masked_scores(
            keys, queries_two, key_marks_ref[...], query_marks_ref[0, :, rows], first_row
        )
        probs = jnp.exp2(scores - lse_ref[0, 0, :, pl.ds(2 * first_row, 2 * QUERY_ROWS)])
        d_probs = lax.dot_general(
            values, grads_two, (((1,), (1,)), ((), ())), preferred_element_type=jnp.float32
        )
        inner = jnp.sum(probs * d_probs, axis=0, keepdims=True)
        d_scores = (probs * (d_probs - inner)).astype(low)
        value_part = lax.dot_general(
            probs.astype(low), grads_two, (((1,), (0,)), ((), ())),
            preferred_element_type=jnp.float32,
        )
        key_part = lax.dot_general(
            d_scores, queries_two, (((1,), (0,)), ((), ())), preferred_element_type=jnp.float32
        )
        if first_row == 0:
            value_sum[...] = value_part
            key_sum[...] = key_part
        else:
            value_sum[...] += value_part
            key_sum[...] += key_part
        query_part = lax.dot_general(
            keys_t, d_scores, (((1,), (0,)), ((), ())), preferred_element_type=jnp.float32
        )
        out_ref[rows, pl.ds(column, 2 * HEAD_DIM)] = (pick_heads(query_part) * 0.125).astype(low)
    out_ref[:, pl.ds(column + width, 2 * HEAD_DIM)] = (key_sum[...] * 0.125).astype(low)
    out_ref[:, pl.ds(column + 2 * width, 2 * HEAD_DIM)] = value_sum[...].astype(low)


def attention_marks(segments, valid_length, shard_index):
    length = segments.shape[1]
    positions = jnp.arange(length, dtype=jnp.int32)
    key_marks = jnp.where(positions[None, :] < valid_length[:, None], segments, -1)

    def own_first(marks):
        return jnp.concatenate(
            own_half_first(marks[:, : length // 2], marks[:, length // 2 :], shard_index), axis=1
        )

    key_marks = jnp.broadcast_to(own_first(key_marks).reshape(-1, 1), (length, 128))
    return key_marks, own_first(segments).reshape(1, 1, length)


def pair_specs(length, pairs, blocks):
    return [
        pl.BlockSpec((length, 2 * HEAD_DIM), lambda s, p, at=at: (s, at * pairs + p))
        for at in blocks
    ]


def attend_forward(qkv, key_marks, query_marks):
    seq_count, _, length = query_marks.shape
    pairs = qkv.shape[1] // (6 * HEAD_DIM)
    return pl.pallas_call(
        forward_body,
        out_shape=(
            jax.ShapeDtypeStruct((qkv.shape[0] // 2, qkv.shape[1] // 3), jnp.bfloat16),
            jax.ShapeDtypeStruct((qkv.shape[0] // 2, qkv.shape[1] // 3), jnp.bfloat16),
            jax.ShapeDtypeStruct((seq_count, pairs, 1, 2 * length), jnp.float32),
        ),
        grid=(seq_count, pairs),
        in_specs=pair_specs(length, pairs, (0, 1, 2))
        + [
            pl.BlockSpec((length, 128), lambda s, p: (s, 0)),
            pl.BlockSpec((1, 1, length), lambda s, p: (s, 0, 0)),
        ],
        out_specs=(
            pl.BlockSpec((length // 2, 2 * HEAD_DIM), lambda s, p: (s, p)),
            pl.BlockSpec((length // 2, 2 * HEAD_DIM), lambda s, p: (s, p)),
            pl.BlockSpec((1, 1, 1, 2 * length), lambda s, p: (s, p, 0, 0)),
        ),
        name="attend_forward",
    )(qkv, qkv, qkv, key_marks, query_marks)


def attend_backward(qkv, own_grad, far_grad, key_marks, query_marks, lse):
    seq_count, _, length = query_marks.shape
    pairs = qkv.shape[1] // (6 * HEAD_DIM)
    return pl.pallas_call(
        backward_body,
        out_shape=jax.ShapeDtypeStruct(qkv.shape, jnp.bfloat16),
        grid=(seq_count, pairs),
        in_specs=pair_specs(length, pairs, (0, 1, 2))
        + [pl.BlockSpec((length // 2, 2 * HEAD_DIM), lambda s, p: (s, p))] * 2
        + [
            pl.BlockSpec((length, 128), lambda s, p: (s, 0)),
            pl.BlockSpec((1, 1, length), lambda s, p: (s, 0, 0)),
            pl.BlockSpec((1, 1, 1, 2 * length), lambda s, p: (s, p, 0, 0)),
        ],
        out_specs=pl.BlockSpec((length, qkv.shape[1]), lambda s, p: (s, 0)),
        scratch_shapes=[pltpu.VMEM((length, 2 * HEAD_DIM), jnp.float32)] * 2,
        name="attend_backward",
    )(qkv, qkv, qkv, own_grad, far_grad, key_marks, query_marks, lse)


def slope_and_gelu(inner):
    rise = 0.5 * (1.0 + lax.erf(inner * 0.7071067811865476))
    density = jnp.exp(-0.5 * inner * inner) * 0.3989422804014327
    return inner * rise, rise + inner * density


def norm_backward(matrix, gain, grad):
    center = matrix - jnp.mean(matrix, axis=-1, keepdims=True)
    spread = jnp.mean(center * center, axis=-1, keepdims=True)
    scale = lax.rsqrt(spread + norm_epsilon)
    normed = center * scale
    d_normed = grad * gain
    pulled = scale * (
        d_normed
        - jnp.mean(d_normed, axis=-1, keepdims=True)
        - normed * jnp.mean(d_normed * normed, axis=-1, keepdims=True)
    )
    return (
        pulled,
        jnp.sum(grad * normed, axis=0),
        jnp.sum(grad, axis=0),
    )


def own_half_first(mine, other, shard_index):
    first = shard_index == 0
    return jnp.where(first, mine, other), jnp.where(first, other, mine)


def mix(left, right, dims):
    return lax.dot_general(left, right, (dims, ((), ())), preferred_element_type=jnp.float32)


def flip(array, bit):
    step = {"x": 1, "core": 2, "y": 4, "xy": 5}[bit]
    return lax.ppermute(array, ("dp", "tensor"), [(i, i ^ step) for i in range(32)])


def turn(array, shift):
    return lax.ppermute(array, "dp", [(i, (i + 4 * shift) % 16) for i in range(16)])


def after(array, done):
    return lax.optimization_barrier((array, done))[0]


def whereabouts():
    index = lax.axis_index("dp")
    return dict(z=index // 4, y=(index // 2) % 2, core=index % 2, x=lax.axis_index("tensor"))


def around_z(block):
    return jnp.stack([block] + [turn(block, shift) for shift in (1, 2, 3)])


def assemble(pieces, place, parts, in_rotation):
    keys = sorted(pieces)
    many_x = 2 if in_rotation or any(key[1] for key in keys) else 1
    rows = pieces[keys[0]].shape[1]
    outs = [
        jax.ShapeDtypeStruct((4, 2, 2, rows, many_x * cols), jnp.bfloat16) for _, cols in parts
    ]

    def put(spot, targets, block, core_off, x_off, y_off):
        core = (spot[2] + core_off) % 2
        y = (spot[1] + y_off) % 2
        for target, (start, cols) in zip(targets, parts):
            target[0, y, core, :, x_off * cols : (x_off + 1) * cols] = block[
                :, start : start + cols
            ]

    def body(spot, *refs):
        sources, targets = refs[: len(keys)], refs[len(keys) :]
        if not in_rotation:
            for number, (core_off, x_off, y_off) in enumerate(keys):
                put(spot, targets, sources[number][0], core_off, x_off, y_off)
            return
        for number, (core_off, shift) in enumerate(keys):

            @pl.when(pl.program_id(0) == shift)
            def _():
                for plane in range(4):
                    block = sources[number][plane]
                    put(spot, targets, block, core_off, plane // 2, plane % 2)

    spot = jnp.stack([place[name] for name in ("z", "y", "core")]).astype(jnp.int32)
    shape = pieces[keys[0]].shape
    if in_rotation:
        piece_spec = pl.BlockSpec(shape, lambda i, spot: (0, 0, 0))
    else:
        piece_spec = pl.BlockSpec((1,) + shape[1:], lambda i, spot: (i, 0, 0))
    results = pl.pallas_call(
        body,
        out_shape=outs,
        grid_spec=pltpu.PrefetchScalarGridSpec(
            num_scalar_prefetch=1,
            grid=(4,),
            in_specs=[piece_spec] * len(keys),
            out_specs=[
                pl.BlockSpec(
                    (1,) + out.shape[1:], lambda i, spot: ((spot[0] + 4 - i) % 4, 0, 0, 0, 0)
                )
                for out in outs
            ],
        ),
        name="assemble",
    )(spot, *[pieces[key] for key in keys])
    return [result.reshape(16 * rows, result.shape[-1]) for result in results]


def side_by_side(*arrays):
    def body(*refs):
        at = 0
        for ref in refs[:-1]:
            refs[-1][:, at : at + ref.shape[1]] = ref[...]
            at += ref.shape[1]

    cols = sum(array.shape[1] for array in arrays)
    return pl.pallas_call(
        body,
        out_shape=jax.ShapeDtypeStruct((arrays[0].shape[0], cols), arrays[0].dtype),
        name="side_by_side",
    )(*arrays)


def project(own, other, weight, bias):
    rows, width = own.shape
    cols = weight.shape[1]

    def body(own_ref, other_ref, weight_ref, bias_ref, out_ref):
        def write(ref):
            product = jnp.dot(ref[...], weight_ref[...], preferred_element_type=jnp.float32)
            out_ref[...] = (product + bias_ref[...]).astype(jnp.bfloat16)

        pl.when(pl.program_id(0) < 2)(lambda: write(own_ref))
        pl.when(pl.program_id(0) >= 2)(lambda: write(other_ref))

    return pl.pallas_call(
        body,
        out_shape=jax.ShapeDtypeStruct((2 * rows, cols), jnp.bfloat16),
        grid=(4,),
        in_specs=[
            pl.BlockSpec((rows // 2, width), lambda i: (jnp.minimum(i, 1), 0)),
            pl.BlockSpec((rows // 2, width), lambda i: (jnp.maximum(i - 2, 0), 0)),
            pl.BlockSpec((width, cols), lambda i: (0, 0)),
            pl.BlockSpec((1, cols), lambda i: (0, 0)),
        ],
        out_specs=pl.BlockSpec((rows // 2, cols), lambda i: (i, 0)),
        name="project",
    )(own, other, weight, bias.reshape(1, cols))


def joined(first, *others):
    total = first.astype(jnp.float32)
    for other in others:
        total = total + other.astype(jnp.float32)
    return total


def other_cores(grad, place):
    blocks = grad.reshape(4, 2, 2, grad.shape[0] // 16, grad.shape[1])
    send = lax.dynamic_index_in_dim(blocks, 1 - place["core"], 2, keepdims=False)
    return blocks, flip(send, "core")


def combine(pairs, place, many_x, z_apart, cut=None):
    rows = pairs[0][0].shape[3]
    widths = [blocks.shape[4] // many_x for blocks, _ in pairs]
    count = len(pairs)

    def body(spot, *refs):
        outs = refs[2 * count :]
        for y_off in range(2):
            y = (spot[1] + y_off) % 2
            at = 0
            for number, cols in enumerate(widths):
                blocks, far = refs[2 * number], refs[2 * number + 1]
                total = blocks[0, y, 0].astype(jnp.float32) + far[0, y].astype(jnp.float32)
                if z_apart:
                    for shift in range(4):

                        @pl.when(pl.program_id(0) == shift)
                        def _():
                            outs[shift][y_off] = total.astype(outs[shift].dtype)

                    continue
                for x_off in range(many_x):
                    place_at = x_off * 2 + y_off
                    part = total[:, x_off * cols : (x_off + 1) * cols]
                    for out, low_end, high_end in ranges(place_at, outs):
                        start, stop = max(at, low_end), min(at + cols, high_end)
                        if start < stop:
                            out[0, :, start - low_end : stop - low_end] = part[
                                :, start - at : stop - at
                            ].astype(out.dtype)
                at += cols

    def ranges(place_at, outs):
        if cut is None:
            return [(outs[place_at], 0, sum(widths))]
        return [
            (outs[2 * place_at], 0, cut),
            (outs[2 * place_at + 1], cut, sum(widths)),
        ]

    spot = jnp.stack([place[name] for name in ("z", "y", "core")]).astype(jnp.int32)
    in_specs = []
    for blocks, _ in pairs:
        n = blocks.shape[4]
        in_specs.append(
            pl.BlockSpec(
                (1, 2, 1, rows, n), lambda i, spot: ((spot[0] + i) % 4, 0, spot[2], 0, 0)
            )
        )
        in_specs.append(
            pl.BlockSpec((1, 2, rows, n), lambda i, spot: ((spot[0] + i) % 4, 0, 0, 0))
        )
    if z_apart:
        shapes = [(2, rows, pairs[0][0].shape[4])] * 4
        out_specs = [pl.BlockSpec(shapes[0], lambda i, spot: (0, 0, 0))] * 4
    else:
        ends = [sum(widths)] if cut is None else [cut, sum(widths) - cut]
        shapes = [(4, rows, cols) for _ in range(2 * many_x) for cols in ends]
        out_specs = [pl.BlockSpec((1,) + shape[1:], lambda i, spot: (i, 0, 0)) for shape in shapes]
    wide = 1 if cut is None else 2
    return pl.pallas_call(
        body,
        out_shape=[
            jax.ShapeDtypeStruct(shape, jnp.bfloat16 if at >= wide else jnp.float32)
            for at, shape in enumerate(shapes)
        ],
        grid_spec=pltpu.PrefetchScalarGridSpec(
            num_scalar_prefetch=1, grid=(4,), in_specs=in_specs, out_specs=out_specs
        ),
        name="combine",
    )(spot, *[array for pair in pairs for array in pair])


def over_z(groups):
    flat = [array for group in groups for array in group]
    rows = flat[0].shape[1]
    cols = sum(group[0].shape[2] for group in groups)

    def body(*refs):
        outs = refs[len(flat) :]
        for shift in range(4):

            @pl.when(pl.program_id(0) == shift)
            def _():
                used = at = 0
                for group in groups:
                    total = joined(*[ref[0] for ref in refs[used : used + len(group)]])
                    used += len(group)
                    outs[shift][:, at : at + total.shape[1]] = total.astype(outs[shift].dtype)
                    at += total.shape[1]

    parts = pl.pallas_call(
        body,
        out_shape=[
            jax.ShapeDtypeStruct((rows, cols), jnp.bfloat16 if shift else jnp.float32)
            for shift in range(4)
        ],
        grid=(4,),
        in_specs=[pl.BlockSpec((1,) + array.shape[1:], lambda i: (i, 0, 0)) for array in flat],
        out_specs=[pl.BlockSpec((rows, cols), lambda i: (0, 0))] * 4,
        name="by_distance",
    )(*flat)
    return joined(parts[0], *[turn(parts[shift], shift) for shift in (1, 2, 3)])


def pack_sums(shard_index, bias_sums, vectors, inner_sums):
    width = vectors[0].shape[0]
    half = width // 2
    wide = inner_sums.shape[0] // 2

    def body(spot, bias_ref, *refs):
        out = refs[-1]
        first = spot[0] == 0
        out[...] = jnp.zeros(out.shape, jnp.float32)
        empty = jnp.zeros((1, half), jnp.float32)
        for row, at in enumerate((0, 2)):
            part = bias_ref[at * half : (at + 1) * half].reshape(1, half)
            out[row : row + 1, :] = jnp.concatenate(
                [jnp.where(first, part, empty), jnp.where(first, empty, part)], axis=1
            )
        for row, ref in enumerate(refs[:-2]):
            out[2 + row : 3 + row, :] = ref[...].reshape(1, width)
        inner = refs[-2][...].reshape(1, 2 * wide)
        mine, far = inner[:, :wide], inner[:, wide:]
        ordered = (jnp.where(first, mine, far), jnp.where(first, far, mine))
        row = 2 + len(refs[:-2])
        for part in ordered:
            for start in range(0, wide, width):
                out[row : row + 1, :] = part[:, start : start + width]
                row += 1

    return pl.pallas_call(
        body,
        out_shape=jax.ShapeDtypeStruct((16, width), jnp.float32),
        in_specs=[pl.BlockSpec(memory_space=pltpu.SMEM)]
        + [pl.BlockSpec(memory_space=pltpu.VMEM)] * (2 + len(vectors)),
        name="pack_sums",
    )(shard_index.reshape(1).astype(jnp.int32), bias_sums, *vectors, inner_sums)


def layer_on_device(
    tokens,
    query_weight,
    query_bias,
    key_weight,
    value_weight,
    value_bias,
    output_weight,
    output_bias,
    first_gain,
    first_shift,
    inner_weight,
    inner_bias,
    outer_weight,
    outer_bias,
    second_gain,
    second_shift,
    segments,
    valid_length,
    cotangent,
):
    low = jnp.bfloat16
    whole = ("tensor", "dp")
    by_links = lax.axis_size("dp") == 16
    place = whereabouts()
    own_rows, width = tokens.shape
    head_cols = query_weight.shape[1]
    hidden_cols = inner_weight.shape[1]
    shard_index = lax.axis_index("tensor")

    other_tokens = flip(tokens, "x")
    packed_qkv = side_by_side(query_weight, key_weight, value_weight)
    packed_in = side_by_side(output_weight.T, inner_weight)
    packed_out = outer_weight.T
    if by_links:
        near_q = around_z(packed_qkv)
        far_q = flip(near_q, "y")
        (full_qkv,) = assemble(
            {
                (0, 0, 0): near_q,
                (0, 0, 1): far_q,
                (1, 0, 0): flip(near_q, "core"),
                (1, 0, 1): flip(far_q, "core"),
            },
            place,
            [(0, 3 * head_cols)],
            False,
        )
        near_a = around_z(after(packed_in, near_q))
        square = jnp.stack([packed_out] + [flip(packed_out, bit) for bit in ("y", "x", "xy")])
        square_z = [square] + [turn(after(square, near_a), shift) for shift in (1, 2, 3)]
        plane_a = [near_a] + [flip(near_a, bit) for bit in ("y", "x")]
    else:
        near_a = None
        full_qkv = lax.all_gather(packed_qkv, "dp", axis=0, tiled=True)
        gathered = lax.all_gather(packed_in, whole, axis=0, tiled=True)
        gathered = gathered.reshape(2, width, head_cols + hidden_cols)
        mine, far = own_half_first(gathered[0], gathered[1], shard_index)
        full_output = jnp.concatenate([mine[:, :head_cols], far[:, :head_cols]], axis=1)
        full_inner = jnp.concatenate([mine[:, head_cols:], far[:, head_cols:]], axis=1)
        gathered = lax.all_gather(packed_out, whole, axis=0, tiled=True)
        gathered = gathered.reshape(2, width, hidden_cols)
        full_outer = jnp.concatenate(
            own_half_first(gathered[0], gathered[1], shard_index), axis=1
        )

    bias_query = lax.dynamic_slice_in_dim(query_bias, shard_index * head_cols, head_cols)
    bias_value = lax.dynamic_slice_in_dim(value_bias, shard_index * head_cols, head_cols)
    bias_qkv = jnp.concatenate([bias_query, jnp.zeros_like(bias_query), bias_value])
    qkv = project(tokens, other_tokens, full_qkv, bias_qkv)
    key_marks, query_marks = attention_marks(segments, valid_length, shard_index)
    own_context, other_context, log_totals = attend_forward(qkv, key_marks, query_marks)
    far_context = flip(other_context, "x")
    if by_links:
        plane_a.append(flip(plane_a[2], "y"))
        pieces = {(0, at // 2, at % 2): piece for at, piece in enumerate(plane_a)}
        pieces.update({(1,) + key[1:]: flip(piece, "core") for key, piece in pieces.items()})
        full_output, full_inner = assemble(
            pieces, place, [(0, head_cols), (head_cols, hidden_cols)], False
        )
        pieces = {(0, shift): piece for shift, piece in enumerate(square_z)}
        pieces.update({(1, shift): flip(piece, "core") for shift, piece in enumerate(square_z)})
        (full_outer,) = assemble(pieces, place, [(0, hidden_cols)], True)
    own_rows_context = jnp.concatenate([own_context, far_context], axis=1)
    attended = mix(own_rows_context, full_output, ((1,), (1,)))
    first_sum = tokens.astype(jnp.float32) + attended + output_bias
    hidden = normalize(first_sum, first_gain, first_shift)
    hidden_low = hidden.astype(low)
    bias_inner = jnp.concatenate(
        own_half_first(inner_bias[:hidden_cols], inner_bias[hidden_cols:], shard_index)
    )
    inner = mix(hidden_low, full_inner, ((1,), (0,))) + bias_inner
    value, slope = slope_and_gelu(inner)
    activated = value.astype(low)
    second_sum = hidden + mix(activated, full_outer, ((1,), (1,))) + outer_bias
    layer_output = normalize(second_sum, second_gain, second_shift).astype(low)
    d_second, second_gain_grad, second_shift_grad = norm_backward(
        second_sum, second_gain, cotangent.astype(jnp.float32)
    )
    outer_bias_grad = jnp.sum(d_second, axis=0)
    d_outer = d_second.astype(low)
    outer_weight_grad = mix(d_outer, activated, ((0,), (0,))).astype(low)
    held_d_outer = after(d_outer, outer_weight_grad)
    d_activated = mix(held_d_outer, full_outer, ((1,), (0,)))
    d_inner = (d_activated * slope).astype(low)
    inner_weight_grad = mix(hidden_low, d_inner, ((0,), (0,))).astype(low)
    inner_bias_grad = jnp.sum(d_inner, axis=0, dtype=jnp.float32)
    through = mix(d_inner, full_inner, ((1,), (1,)))
    d_hidden = d_second + through
    d_first, first_gain_grad, first_shift_grad = norm_backward(first_sum, first_gain, d_hidden)
    output_bias_grad = jnp.sum(d_first, axis=0)
    d_attended = d_first.astype(low)
    output_weight_grad = mix(d_attended, own_rows_context, ((0,), (0,))).astype(low)
    d_own_context = mix(d_attended, full_output, ((1,), (0,))).astype(low)
    far_d_context = flip(d_own_context[:, head_cols:], "x")
    if by_links:
        square_b = combine([other_cores(outer_weight_grad, place)], place, 2, True)
        turned_b = [square_b[0]] + [turn(square_b[shift], shift) for shift in (1, 2, 3)]
        plane_a = combine(
            [other_cores(output_weight_grad, place), other_cores(inner_weight_grad, place)],
            place,
            2,
            False,
            cut=1024,
        )
        far_a = (flip(plane_a[6], "y"), flip(plane_a[7], "x"))
        near_a = (flip(plane_a[2], "y"), flip(plane_a[5], "x"))
    d_qkv = attend_backward(
        qkv, d_own_context, far_d_context, key_marks, query_marks, log_totals)
    if by_links:
        late_a = (
            flip(joined(plane_a[4], far_a[0]).astype(low), "x"),
            flip(joined(plane_a[3], far_a[1]).astype(low), "y"),
        )
    qkv_weight_grad = (
        mix(tokens, d_qkv[:own_rows], ((0,), (0,)))
        + mix(other_tokens, d_qkv[own_rows:], ((0,), (0,)))
    ).astype(low)
    held_d_qkv = after(d_qkv, qkv_weight_grad)
    partial_input = mix(held_d_qkv, full_qkv, ((1,), (1,)))
    if by_links:

        def part_b(x_off, y_off=None):
            rows = slice(None) if y_off is None else y_off
            columns = slice(x_off * hidden_cols, (x_off + 1) * hidden_cols)
            return joined(*[rows_b[rows, :, columns] for rows_b in turned_b])

        far_b = flip(part_b(1).astype(low), "x")
    far_input = flip(partial_input[own_rows:].astype(low), "x")
    input_gradient = d_first + partial_input[:own_rows] + far_input.astype(jnp.float32)

    def scatter(grad, axes, cols):
        if grad.shape[1] > cols:
            grad = jnp.concatenate(
                own_half_first(grad[:, :cols], grad[:, cols:], shard_index), axis=0
            )
        return lax.psum_scatter(grad, axes, scatter_dimension=0, tiled=True).astype(jnp.float32)

    bias_local = jnp.sum(held_d_qkv, axis=0, dtype=jnp.float32)
    local = pack_sums(
        shard_index,
        bias_local,
        [
            output_bias_grad,
            first_gain_grad,
            first_shift_grad,
            outer_bias_grad,
            second_gain_grad,
            second_shift_grad,
        ],
        inner_bias_grad,
    )
    if by_links:
        local = local + flip(local, "core")
        plane_q = combine([other_cores(qkv_weight_grad, place)], place, 1, False)
        far_q = flip(plane_q[1], "y")
        met = [flip(local, bit) for bit in ("x", "y", "xy")]
        local = (local + met[0]) + (met[1] + met[2])
        qkv_shard = over_z([(plane_q[0], far_q)])
        turned = [turn(local, shift) for shift in (1, 2, 3)]
        summed = (local + turned[1]) + (turned[0] + turned[2])
        both = over_z([(plane_a[at], near_a[at], late_a[at]) for at in range(2)])
        output_shard, inner_shard = both[:, :head_cols].T, both[:, head_cols:]

        outer_shard = joined(
            part_b(0, 0),
            far_b[0],
            flip(joined(part_b(0, 1), far_b[1]).astype(low), "y"),
        ).T
    else:
        outer_shard = scatter(outer_weight_grad, whole, hidden_cols).T
        inner_shard = scatter(inner_weight_grad, whole, hidden_cols)
        output_shard = scatter(output_weight_grad, whole, head_cols).T
        qkv_shard = scatter(qkv_weight_grad, ("dp",), 3 * head_cols)
        summed = lax.psum(local, ("dp", "tensor"))
    rows = [summed[at] for at in range(8)]
    return (
        layer_output,
        input_gradient,
        qkv_shard[:, :head_cols],
        rows[0],
        qkv_shard[:, head_cols : 2 * head_cols],
        qkv_shard[:, 2 * head_cols :],
        rows[1],
        output_shard,
        rows[2],
        rows[3],
        rows[4],
        inner_shard,
        summed[8:12].reshape(-1),
        outer_shard,
        rows[5],
        rows[6],
        rows[7],
    )


def solution(mesh):
    placed = (
        P(("dp", "tensor"), None),
        P("dp", "tensor"),
        P(),
        P("dp", "tensor"),
        P("dp", "tensor"),
        P(),
        P("tensor", "dp"),
        P(),
        P(),
        P(),
        P("dp", "tensor"),
        P(),
        P("tensor", "dp"),
        P(),
        P(),
        P(),
        P("dp", None),
        P("dp"),
        P(("dp", "tensor"), None),
    )
    return jax.shard_map(
        layer_on_device,
        mesh=mesh,
        in_specs=placed,
        out_specs=(
            P(("dp", "tensor"), None),
            P(("dp", "tensor"), None),
            P("dp", "tensor"),
            P(),
            P("dp", "tensor"),
            P("dp", "tensor"),
            P(),
            P("tensor", "dp"),
            P(),
            P(),
            P(),
            P("dp", "tensor"),
            P(),
            P("tensor", "dp"),
            P(),
            P(),
            P(),
        ),
        check_vma=False,
    )
```

```python
import jax
import jax.numpy as jnp
from jax import lax
from jax.experimental import pallas as pl
from jax.experimental.pallas import tpu as pltpu
from jax.sharding import PartitionSpec as P

HEAD_DIM = 64


norm_epsilon = 1e-12
masked_score = -1e30


def normalize(matrix, gain, shift):
    center = matrix - jnp.mean(matrix, axis=-1, keepdims=True)
    spread = jnp.mean(center * center, axis=-1, keepdims=True)
    return center * lax.rsqrt(spread + norm_epsilon) * gain + shift


LOG2_E = 1.4426950408889634
QUERY_ROWS = 256


def two_heads(rows):
    lane = lax.broadcasted_iota(jnp.int32, rows.shape, 1)
    zero = jnp.zeros_like(rows)
    return jnp.concatenate(
        [jnp.where(lane < HEAD_DIM, rows, zero), jnp.where(lane < HEAD_DIM, zero, rows)], axis=0
    )


def pick_heads(columns):
    count = columns.shape[1] // 2
    row = lax.broadcasted_iota(jnp.int32, (columns.shape[0], count), 0)
    return jnp.where(row < HEAD_DIM, columns[:, :count], columns[:, count:]).T


def masked_scores(keys, queries_two, key_marks, query_marks, first_row):
    scores = lax.dot_general(
        keys, queries_two, (((1,), (1,)), ((), ())), preferred_element_type=jnp.float32
    ) * (0.125 * LOG2_E)
    count = queries_two.shape[0] // 2
    length = keys.shape[0]
    query_two = jnp.concatenate([query_marks, query_marks], axis=1)
    marks = jnp.concatenate([key_marks] * (2 * count // key_marks.shape[1]), axis=1)
    allowed = marks == query_two
    pieces = []
    for start in range(0, length, count):
        part = allowed[start : start + count]
        if start == first_row:
            row = lax.broadcasted_iota(jnp.int32, (count, 2 * count), 0)
            column = lax.broadcasted_iota(jnp.int32, (count, 2 * count), 1)
            part = part | (row == jnp.where(column < count, column, column - count))
        pieces.append(jnp.where(part, scores[start : start + count], masked_score))
    return jnp.concatenate(pieces, axis=0)


def forward_body(
    query_ref, key_ref, value_ref, key_marks_ref, query_marks_ref, own_ref, other_ref, lse_ref
):
    length = key_ref.shape[0]
    keys = key_ref[...]
    values_t = value_ref[...].T
    for first_row in range(0, length, QUERY_ROWS):
        rows = pl.ds(first_row, QUERY_ROWS)
        scores = masked_scores(
            keys,
            two_heads(query_ref[rows, :]),
            key_marks_ref[...],
            query_marks_ref[0, :, rows],
            first_row,
        )
        largest = jnp.max(scores, axis=0, keepdims=True)
        powers = jnp.exp2(scores - largest)
        totals = jnp.sum(powers, axis=0, keepdims=True)
        product = lax.dot_general(
            values_t,
            powers.astype(jnp.bfloat16),
            (((1,), (0,)), ((), ())),
            preferred_element_type=jnp.float32,
        )
        target = own_ref if first_row < length // 2 else other_ref
        target[pl.ds(first_row % (length // 2), QUERY_ROWS), :] = pick_heads(
            product * (1.0 / totals)
        ).astype(jnp.bfloat16)
        lse_ref[0, 0, :, pl.ds(2 * first_row, 2 * QUERY_ROWS)] = largest + jnp.log2(totals)


def backward_body(
    query_ref, key_ref, value_ref, own_ref, far_ref, key_marks_ref, query_marks_ref, lse_ref, out_ref,
    key_sum, value_sum,
):
    length = key_ref.shape[0]
    width = out_ref.shape[1] // 3
    low = jnp.bfloat16
    keys = key_ref[...]
    values = value_ref[...]
    keys_t = keys.T
    column = pl.multiple_of(pl.program_id(1) * 2 * HEAD_DIM, 2 * HEAD_DIM)
    for first_row in range(0, length, QUERY_ROWS):
        rows = pl.ds(first_row, QUERY_ROWS)
        queries_two = two_heads(query_ref[rows, :])
        grad_ref = own_ref if first_row < length // 2 else far_ref
        grads_two = two_heads(grad_ref[pl.ds(first_row % (length // 2), QUERY_ROWS), :])
        scores = masked_scores(
            keys, queries_two, key_marks_ref[...], query_marks_ref[0, :, rows], first_row
        )
        probs = jnp.exp2(scores - lse_ref[0, 0, :, pl.ds(2 * first_row, 2 * QUERY_ROWS)])
        d_probs = lax.dot_general(
            values, grads_two, (((1,), (1,)), ((), ())), preferred_element_type=jnp.float32
        )
        inner = jnp.sum(probs * d_probs, axis=0, keepdims=True)
        d_scores = (probs * (d_probs - inner)).astype(low)
        value_part = lax.dot_general(
            probs.astype(low), grads_two, (((1,), (0,)), ((), ())),
            preferred_element_type=jnp.float32,
        )
        key_part = lax.dot_general(
            d_scores, queries_two, (((1,), (0,)), ((), ())), preferred_element_type=jnp.float32
        )
        if first_row == 0:
            value_sum[...] = value_part
            key_sum[...] = key_part
        else:
            value_sum[...] += value_part
            key_sum[...] += key_part
        query_part = lax.dot_general(
            keys_t, d_scores, (((1,), (0,)), ((), ())), preferred_element_type=jnp.float32
        )
        out_ref[rows, pl.ds(column, 2 * HEAD_DIM)] = (pick_heads(query_part) * 0.125).astype(low)
    out_ref[:, pl.ds(column + width, 2 * HEAD_DIM)] = (key_sum[...] * 0.125).astype(low)
    out_ref[:, pl.ds(column + 2 * width, 2 * HEAD_DIM)] = value_sum[...].astype(low)


def attention_marks(segments, valid_length, shard_index):
    length = segments.shape[1]
    positions = jnp.arange(length, dtype=jnp.int32)
    key_marks = jnp.where(positions[None, :] < valid_length[:, None], segments, -1)

    def own_first(marks):
        return jnp.concatenate(
            own_half_first(marks[:, : length // 2], marks[:, length // 2 :], shard_index), axis=1
        )

    key_marks = jnp.broadcast_to(own_first(key_marks).reshape(-1, 1), (length, 128))
    return key_marks, own_first(segments).reshape(1, 1, length)


def pair_specs(length, pairs, blocks):
    return [
        pl.BlockSpec((length, 2 * HEAD_DIM), lambda s, p, at=at: (s, at * pairs + p))
        for at in blocks
    ]


def attend_forward(qkv, key_marks, query_marks):
    seq_count, _, length = query_marks.shape
    pairs = qkv.shape[1] // (6 * HEAD_DIM)
    return pl.pallas_call(
        forward_body,
        out_shape=(
            jax.ShapeDtypeStruct((qkv.shape[0] // 2, qkv.shape[1] // 3), jnp.bfloat16),
            jax.ShapeDtypeStruct((qkv.shape[0] // 2, qkv.shape[1] // 3), jnp.bfloat16),
            jax.ShapeDtypeStruct((seq_count, pairs, 1, 2 * length), jnp.float32),
        ),
        grid=(seq_count, pairs),
        in_specs=pair_specs(length, pairs, (0, 1, 2))
        + [
            pl.BlockSpec((length, 128), lambda s, p: (s, 0)),
            pl.BlockSpec((1, 1, length), lambda s, p: (s, 0, 0)),
        ],
        out_specs=(
            pl.BlockSpec((length // 2, 2 * HEAD_DIM), lambda s, p: (s, p)),
            pl.BlockSpec((length // 2, 2 * HEAD_DIM), lambda s, p: (s, p)),
            pl.BlockSpec((1, 1, 1, 2 * length), lambda s, p: (s, p, 0, 0)),
        ),
    )(qkv, qkv, qkv, key_marks, query_marks)


def attend_backward(qkv, own_grad, far_grad, key_marks, query_marks, lse):
    seq_count, _, length = query_marks.shape
    pairs = qkv.shape[1] // (6 * HEAD_DIM)
    return pl.pallas_call(
        backward_body,
        out_shape=jax.ShapeDtypeStruct(qkv.shape, jnp.bfloat16),
        grid=(seq_count, pairs),
        in_specs=pair_specs(length, pairs, (0, 1, 2))
        + [pl.BlockSpec((length // 2, 2 * HEAD_DIM), lambda s, p: (s, p))] * 2
        + [
            pl.BlockSpec((length, 128), lambda s, p: (s, 0)),
            pl.BlockSpec((1, 1, length), lambda s, p: (s, 0, 0)),
            pl.BlockSpec((1, 1, 1, 2 * length), lambda s, p: (s, p, 0, 0)),
        ],
        out_specs=pl.BlockSpec((length, qkv.shape[1]), lambda s, p: (s, 0)),
        scratch_shapes=[pltpu.VMEM((length, 2 * HEAD_DIM), jnp.float32)] * 2,
    )(qkv, qkv, qkv, own_grad, far_grad, key_marks, query_marks, lse)


def slope_and_gelu(inner):
    rise = 0.5 * (1.0 + lax.erf(inner * 0.7071067811865476))
    density = jnp.exp(-0.5 * inner * inner) * 0.3989422804014327
    return inner * rise, rise + inner * density


def norm_backward(matrix, gain, grad):
    center = matrix - jnp.mean(matrix, axis=-1, keepdims=True)
    spread = jnp.mean(center * center, axis=-1, keepdims=True)
    scale = lax.rsqrt(spread + norm_epsilon)
    normed = center * scale
    d_normed = grad * gain
    pulled = scale * (
        d_normed
        - jnp.mean(d_normed, axis=-1, keepdims=True)
        - normed * jnp.mean(d_normed * normed, axis=-1, keepdims=True)
    )
    return (
        pulled,
        jnp.sum(grad * normed, axis=0),
        jnp.sum(grad, axis=0),
    )


def own_half_first(mine, other, shard_index):
    first = shard_index == 0
    return jnp.where(first, mine, other), jnp.where(first, other, mine)


def mix(left, right, dims):
    return lax.dot_general(left, right, (dims, ((), ())), preferred_element_type=jnp.float32)


def flip(array, bit):
    step = {"x": 1, "core": 2, "y": 4, "xy": 5}[bit]
    return lax.ppermute(array, ("dp", "tensor"), [(i, i ^ step) for i in range(32)])


def turn(array, shift):
    return lax.ppermute(array, "dp", [(i, (i + 4 * shift) % 16) for i in range(16)])


def after(array, done):
    return lax.optimization_barrier((array, done))[0]


def whereabouts():
    index = lax.axis_index("dp")
    return dict(z=index // 4, y=(index // 2) % 2, core=index % 2, x=lax.axis_index("tensor"))


def around_z(block):
    return jnp.stack([block] + [turn(block, shift) for shift in (1, 2, 3)])


def assemble(pieces, place, parts, in_rotation):
    keys = sorted(pieces)
    many_x = 2 if in_rotation or any(key[1] for key in keys) else 1
    rows = pieces[keys[0]].shape[1]
    outs = [
        jax.ShapeDtypeStruct((4, 2, 2, rows, many_x * cols), jnp.bfloat16) for _, cols in parts
    ]

    def put(spot, targets, block, core_off, x_off, y_off):
        core = (spot[2] + core_off) % 2
        y = (spot[1] + y_off) % 2
        for target, (start, cols) in zip(targets, parts):
            target[0, y, core, :, x_off * cols : (x_off + 1) * cols] = block[
                :, start : start + cols
            ]

    def body(spot, *refs):
        sources, targets = refs[: len(keys)], refs[len(keys) :]
        if not in_rotation:
            for number, (core_off, x_off, y_off) in enumerate(keys):
                put(spot, targets, sources[number][0], core_off, x_off, y_off)
            return
        for number, (core_off, shift) in enumerate(keys):

            @pl.when(pl.program_id(0) == shift)
            def _():
                for plane in range(4):
                    block = sources[number][plane]
                    put(spot, targets, block, core_off, plane // 2, plane % 2)

    spot = jnp.stack([place[name] for name in ("z", "y", "core")]).astype(jnp.int32)
    shape = pieces[keys[0]].shape
    if in_rotation:
        piece_spec = pl.BlockSpec(shape, lambda i, spot: (0, 0, 0))
    else:
        piece_spec = pl.BlockSpec((1,) + shape[1:], lambda i, spot: (i, 0, 0))
    results = pl.pallas_call(
        body,
        out_shape=outs,
        grid_spec=pltpu.PrefetchScalarGridSpec(
            num_scalar_prefetch=1,
            grid=(4,),
            in_specs=[piece_spec] * len(keys),
            out_specs=[
                pl.BlockSpec(
                    (1,) + out.shape[1:], lambda i, spot: ((spot[0] + 4 - i) % 4, 0, 0, 0, 0)
                )
                for out in outs
            ],
        ),
    )(spot, *[pieces[key] for key in keys])
    return [result.reshape(16 * rows, result.shape[-1]) for result in results]


def side_by_side(*arrays):
    def body(*refs):
        at = 0
        for ref in refs[:-1]:
            refs[-1][:, at : at + ref.shape[1]] = ref[...]
            at += ref.shape[1]

    cols = sum(array.shape[1] for array in arrays)
    return pl.pallas_call(
        body,
        out_shape=jax.ShapeDtypeStruct((arrays[0].shape[0], cols), arrays[0].dtype),
    )(*arrays)


def project(own, other, pieces, place, bias):
    rows, width = own.shape
    keys = sorted(pieces)
    cols = pieces[keys[0]].shape[2]
    high = width // 16

    def body(spot, own_ref, other_ref, bias_ref, *refs):
        sources, weight_ref, out_ref = refs[:-2], refs[-2], refs[-1]

        @pl.when(pl.program_id(0) == 0)
        def _():
            for ref, (core_off, _, y_off) in zip(sources, keys):
                core, y = (spot[2] + core_off) % 2, (spot[1] + y_off) % 2
                for shift in range(4):
                    weight_ref[(spot[0] + 4 - shift) % 4, y, core] = ref[shift]

        weight = weight_ref[...].reshape(width, cols)

        def write(ref):
            product = jnp.dot(ref[...], weight, preferred_element_type=jnp.float32)
            out_ref[...] = (product + bias_ref[...]).astype(jnp.bfloat16)

        pl.when(pl.program_id(0) < 2)(lambda: write(own_ref))
        pl.when(pl.program_id(0) >= 2)(lambda: write(other_ref))

    spot = jnp.stack([place["z"], place["y"], place["core"]]).astype(jnp.int32)
    weight, out = pl.pallas_call(
        body,
        out_shape=[
            jax.ShapeDtypeStruct((4, 2, 2, high, cols), jnp.bfloat16),
            jax.ShapeDtypeStruct((2 * rows, cols), jnp.bfloat16),
        ],
        grid_spec=pltpu.PrefetchScalarGridSpec(
            num_scalar_prefetch=1,
            grid=(4,),
            in_specs=[
                pl.BlockSpec((rows // 2, width), lambda i, spot: (jnp.minimum(i, 1), 0)),
                pl.BlockSpec((rows // 2, width), lambda i, spot: (jnp.maximum(i - 2, 0), 0)),
                pl.BlockSpec((1, cols), lambda i, spot: (0, 0)),
            ]
            + [pl.BlockSpec((4, high, cols), lambda i, spot: (0, 0, 0))] * len(keys),
            out_specs=[
                pl.BlockSpec((4, 2, 2, high, cols), lambda i, spot: (0, 0, 0, 0, 0)),
                pl.BlockSpec((rows // 2, cols), lambda i, spot: (i, 0)),
            ],
        ),
    )(spot, own, other, bias.reshape(1, cols), *[pieces[key] for key in keys])
    return weight.reshape(width, cols), out


def joined(first, *others):
    total = first.astype(jnp.float32)
    for other in others:
        total = total + other.astype(jnp.float32)
    return total


def other_cores(grad, place):
    blocks = grad.reshape(4, 2, 2, grad.shape[0] // 16, grad.shape[1])
    send = lax.dynamic_index_in_dim(blocks, 1 - place["core"], 2, keepdims=False)
    return blocks, flip(send, "core")


def combine(pairs, place, many_x, z_apart, cut=None):
    rows = pairs[0][0].shape[3]
    widths = [blocks.shape[4] // many_x for blocks, _ in pairs]
    count = len(pairs)

    def body(spot, *refs):
        outs = refs[2 * count :]
        for y_off in range(2):
            y = (spot[1] + y_off) % 2
            at = 0
            for number, cols in enumerate(widths):
                blocks, far = refs[2 * number], refs[2 * number + 1]
                total = blocks[0, y, 0].astype(jnp.float32) + far[0, y].astype(jnp.float32)
                if z_apart:
                    for shift in range(4):

                        @pl.when(pl.program_id(0) == shift)
                        def _():
                            outs[shift][y_off] = total.astype(outs[shift].dtype)

                    continue
                for x_off in range(many_x):
                    place_at = x_off * 2 + y_off
                    part = total[:, x_off * cols : (x_off + 1) * cols]
                    for out, low_end, high_end in ranges(place_at, outs):
                        start, stop = max(at, low_end), min(at + cols, high_end)
                        if start < stop:
                            out[0, :, start - low_end : stop - low_end] = part[
                                :, start - at : stop - at
                            ].astype(out.dtype)
                at += cols

    def ranges(place_at, outs):
        if cut is None:
            return [(outs[place_at], 0, sum(widths))]
        return [
            (outs[2 * place_at], 0, cut),
            (outs[2 * place_at + 1], cut, sum(widths)),
        ]

    spot = jnp.stack([place[name] for name in ("z", "y", "core")]).astype(jnp.int32)
    in_specs = []
    for blocks, _ in pairs:
        n = blocks.shape[4]
        in_specs.append(
            pl.BlockSpec(
                (1, 2, 1, rows, n), lambda i, spot: ((spot[0] + i) % 4, 0, spot[2], 0, 0)
            )
        )
        in_specs.append(
            pl.BlockSpec((1, 2, rows, n), lambda i, spot: ((spot[0] + i) % 4, 0, 0, 0))
        )
    if z_apart:
        shapes = [(2, rows, pairs[0][0].shape[4])] * 4
        out_specs = [pl.BlockSpec(shapes[0], lambda i, spot: (0, 0, 0))] * 4
    else:
        ends = [sum(widths)] if cut is None else [cut, sum(widths) - cut]
        shapes = [(4, rows, cols) for _ in range(2 * many_x) for cols in ends]
        out_specs = [pl.BlockSpec((1,) + shape[1:], lambda i, spot: (i, 0, 0)) for shape in shapes]
    wide = 1 if cut is None else 2
    return pl.pallas_call(
        body,
        out_shape=[
            jax.ShapeDtypeStruct(shape, jnp.bfloat16 if at >= wide else jnp.float32)
            for at, shape in enumerate(shapes)
        ],
        grid_spec=pltpu.PrefetchScalarGridSpec(
            num_scalar_prefetch=1, grid=(4,), in_specs=in_specs, out_specs=out_specs
        ),
    )(spot, *[array for pair in pairs for array in pair])


def over_z(groups):
    flat = [array for group in groups for array in group]
    rows = flat[0].shape[1]
    cols = sum(group[0].shape[2] for group in groups)

    def body(*refs):
        outs = refs[len(flat) :]
        for shift in range(4):

            @pl.when(pl.program_id(0) == shift)
            def _():
                used = at = 0
                for group in groups:
                    total = joined(*[ref[0] for ref in refs[used : used + len(group)]])
                    used += len(group)
                    outs[shift][:, at : at + total.shape[1]] = total.astype(outs[shift].dtype)
                    at += total.shape[1]

    parts = pl.pallas_call(
        body,
        out_shape=[
            jax.ShapeDtypeStruct((rows, cols), jnp.bfloat16 if shift else jnp.float32)
            for shift in range(4)
        ],
        grid=(4,),
        in_specs=[pl.BlockSpec((1,) + array.shape[1:], lambda i: (i, 0, 0)) for array in flat],
        out_specs=[pl.BlockSpec((rows, cols), lambda i: (0, 0))] * 4,
    )(*flat)
    arrived = [turn(parts[shift], shift) for shift in (1, 2, 3)]
    return joined(parts[0], *arrived)


def pack_sums(shard_index, bias_sums, vectors, inner_sums):
    width = vectors[0].shape[0]
    half = width // 2
    wide = inner_sums.shape[0] // 2

    def body(spot, bias_ref, *refs):
        out = refs[-1]
        first = spot[0] == 0
        out[...] = jnp.zeros(out.shape, jnp.float32)
        empty = jnp.zeros((1, half), jnp.float32)
        for row, at in enumerate((0, 2)):
            part = bias_ref[at * half : (at + 1) * half].reshape(1, half)
            out[row : row + 1, :] = jnp.concatenate(
                [jnp.where(first, part, empty), jnp.where(first, empty, part)], axis=1
            )
        for row, ref in enumerate(refs[:-2]):
            out[2 + row : 3 + row, :] = ref[...].reshape(1, width)
        inner = refs[-2][...].reshape(1, 2 * wide)
        mine, far = inner[:, :wide], inner[:, wide:]
        ordered = (jnp.where(first, mine, far), jnp.where(first, far, mine))
        row = 2 + len(refs[:-2])
        for part in ordered:
            for start in range(0, wide, width):
                out[row : row + 1, :] = part[:, start : start + width]
                row += 1

    return pl.pallas_call(
        body,
        out_shape=jax.ShapeDtypeStruct((16, width), jnp.float32),
        in_specs=[pl.BlockSpec(memory_space=pltpu.SMEM)]
        + [pl.BlockSpec(memory_space=pltpu.VMEM)] * (2 + len(vectors)),
    )(shard_index.reshape(1).astype(jnp.int32), bias_sums, *vectors, inner_sums)


def layer_on_device(
    tokens,
    query_weight,
    query_bias,
    key_weight,
    value_weight,
    value_bias,
    output_weight,
    output_bias,
    first_gain,
    first_shift,
    inner_weight,
    inner_bias,
    outer_weight,
    outer_bias,
    second_gain,
    second_shift,
    segments,
    valid_length,
    cotangent,
):
    low = jnp.bfloat16
    whole = ("tensor", "dp")
    by_links = lax.axis_size("dp") == 16
    place = whereabouts()
    own_rows, width = tokens.shape
    head_cols = query_weight.shape[1]
    hidden_cols = inner_weight.shape[1]
    shard_index = lax.axis_index("tensor")

    other_tokens = flip(tokens, "x")
    packed_qkv = side_by_side(query_weight, key_weight, value_weight)
    packed_in = side_by_side(output_weight.T, inner_weight)
    packed_out = outer_weight.T
    if by_links:
        near_q = around_z(packed_qkv)
        far_q = flip(near_q, "y")
        pieces_q = {
            (0, 0, 0): near_q,
            (0, 0, 1): far_q,
            (1, 0, 0): flip(near_q, "core"),
            (1, 0, 1): flip(far_q, "core"),
        }
        near_a = around_z(after(packed_in, near_q))
        square = jnp.stack([packed_out] + [flip(packed_out, bit) for bit in ("y", "x", "xy")])
        square_z = [square] + [turn(after(square, near_a), shift) for shift in (1, 2, 3)]
        plane_a = [near_a] + [flip(near_a, bit) for bit in ("y", "x")]
    else:
        near_a = None
        full_qkv = lax.all_gather(packed_qkv, "dp", axis=0, tiled=True)
        gathered = lax.all_gather(packed_in, whole, axis=0, tiled=True)
        gathered = gathered.reshape(2, width, head_cols + hidden_cols)
        mine, far = own_half_first(gathered[0], gathered[1], shard_index)
        full_output = jnp.concatenate([mine[:, :head_cols], far[:, :head_cols]], axis=1)
        full_inner = jnp.concatenate([mine[:, head_cols:], far[:, head_cols:]], axis=1)
        gathered = lax.all_gather(packed_out, whole, axis=0, tiled=True)
        gathered = gathered.reshape(2, width, hidden_cols)
        full_outer = jnp.concatenate(
            own_half_first(gathered[0], gathered[1], shard_index), axis=1
        )

    bias_query = lax.dynamic_slice_in_dim(query_bias, shard_index * head_cols, head_cols)
    bias_value = lax.dynamic_slice_in_dim(value_bias, shard_index * head_cols, head_cols)
    bias_qkv = jnp.concatenate([bias_query, jnp.zeros_like(bias_query), bias_value])
    if by_links:
        full_qkv, qkv = project(tokens, other_tokens, pieces_q, place, bias_qkv)
    else:
        rows_all = jnp.concatenate([tokens, other_tokens], axis=0)
        qkv = (mix(rows_all, full_qkv, ((1,), (0,))) + bias_qkv).astype(low)
    key_marks, query_marks = attention_marks(segments, valid_length, shard_index)
    own_context, other_context, log_totals = attend_forward(qkv, key_marks, query_marks)
    far_context = flip(other_context, "x")
    if by_links:
        plane_a.append(flip(plane_a[2], "y"))
        pieces = {(0, at // 2, at % 2): piece for at, piece in enumerate(plane_a)}
        pieces.update({(1,) + key[1:]: flip(piece, "core") for key, piece in pieces.items()})
        full_output, full_inner = assemble(
            pieces, place, [(0, head_cols), (head_cols, hidden_cols)], False
        )
        pieces = {(0, shift): piece for shift, piece in enumerate(square_z)}
        pieces.update({(1, shift): flip(piece, "core") for shift, piece in enumerate(square_z)})
        (full_outer,) = assemble(pieces, place, [(0, hidden_cols)], True)
    own_rows_context = jnp.concatenate([own_context, far_context], axis=1)
    attended = mix(own_rows_context, full_output, ((1,), (1,)))
    first_sum = tokens.astype(jnp.float32) + attended + output_bias
    hidden = normalize(first_sum, first_gain, first_shift)
    hidden_low = hidden.astype(low)
    bias_inner = jnp.concatenate(
        own_half_first(inner_bias[:hidden_cols], inner_bias[hidden_cols:], shard_index)
    )
    inner = mix(hidden_low, full_inner, ((1,), (0,))) + bias_inner
    value, slope = slope_and_gelu(inner)
    activated = value.astype(low)
    second_sum = hidden + mix(activated, full_outer, ((1,), (1,))) + outer_bias
    layer_output = normalize(second_sum, second_gain, second_shift).astype(low)
    d_second, second_gain_grad, second_shift_grad = norm_backward(
        second_sum, second_gain, cotangent.astype(jnp.float32)
    )
    outer_bias_grad = jnp.sum(d_second, axis=0)
    d_outer = d_second.astype(low)
    outer_weight_grad = mix(d_outer, activated, ((0,), (0,))).astype(low)
    held_d_outer = after(d_outer, outer_weight_grad)
    d_activated = mix(held_d_outer, full_outer, ((1,), (0,)))
    d_inner = (d_activated * slope).astype(low)
    inner_weight_grad = mix(hidden_low, d_inner, ((0,), (0,))).astype(low)
    inner_bias_grad = jnp.sum(d_inner, axis=0, dtype=jnp.float32)
    through = mix(d_inner, full_inner, ((1,), (1,)))
    d_hidden = d_second + through
    d_first, first_gain_grad, first_shift_grad = norm_backward(first_sum, first_gain, d_hidden)
    output_bias_grad = jnp.sum(d_first, axis=0)
    d_attended = d_first.astype(low)
    output_weight_grad = mix(d_attended, own_rows_context, ((0,), (0,))).astype(low)
    d_own_context = mix(d_attended, full_output, ((1,), (0,))).astype(low)
    far_d_context = flip(d_own_context[:, head_cols:], "x")
    if by_links:
        square_b = combine([other_cores(outer_weight_grad, place)], place, 2, True)
        turned_b = [square_b[0]] + [turn(square_b[shift], shift) for shift in (1, 2, 3)]
        plane_a = combine(
            [other_cores(output_weight_grad, place), other_cores(inner_weight_grad, place)],
            place,
            2,
            False,
            cut=1024,
        )
        far_a = (flip(plane_a[6], "y"), flip(plane_a[7], "x"))
        near_a = (flip(plane_a[2], "y"), flip(plane_a[5], "x"))
    d_qkv = attend_backward(
        qkv, d_own_context, far_d_context, key_marks, query_marks, log_totals)
    if by_links:
        late_a = (
            flip(joined(plane_a[4], far_a[0]).astype(low), "x"),
            flip(joined(plane_a[3], far_a[1]).astype(low), "y"),
        )
    qkv_weight_grad = (
        mix(tokens, d_qkv[:own_rows], ((0,), (0,)))
        + mix(other_tokens, d_qkv[own_rows:], ((0,), (0,)))
    ).astype(low)
    held_d_qkv = after(d_qkv, qkv_weight_grad)
    partial_input = mix(held_d_qkv, full_qkv, ((1,), (1,)))
    if by_links:

        def part_b(x_off, y_off=None):
            rows = slice(None) if y_off is None else y_off
            columns = slice(x_off * hidden_cols, (x_off + 1) * hidden_cols)
            return joined(*[rows_b[rows, :, columns] for rows_b in turned_b])

        far_b = flip(part_b(1).astype(low), "x")
    far_input = flip(partial_input[own_rows:].astype(low), "x")
    input_gradient = d_first + partial_input[:own_rows] + far_input.astype(jnp.float32)

    def scatter(grad, axes, cols):
        if grad.shape[1] > cols:
            grad = jnp.concatenate(
                own_half_first(grad[:, :cols], grad[:, cols:], shard_index), axis=0
            )
        return lax.psum_scatter(grad, axes, scatter_dimension=0, tiled=True).astype(jnp.float32)

    bias_local = jnp.sum(d_qkv, axis=0, dtype=jnp.float32)
    local = pack_sums(
        shard_index,
        bias_local,
        [
            output_bias_grad,
            first_gain_grad,
            first_shift_grad,
            outer_bias_grad,
            second_gain_grad,
            second_shift_grad,
        ],
        inner_bias_grad,
    )
    if by_links:
        local = local + flip(local, "core")
        plane_q = combine([other_cores(qkv_weight_grad, place)], place, 1, False)
        far_q = flip(plane_q[1], "y")
        met = [flip(local, bit) for bit in ("x", "y", "xy")]
        local = (local + met[0]) + (met[1] + met[2])
        qkv_shard = over_z([(plane_q[0], far_q)])
        turned = [turn(local, shift) for shift in (1, 2, 3)]
        summed = (local + turned[1]) + (turned[0] + turned[2])
        both = over_z([(plane_a[at], near_a[at], late_a[at]) for at in range(2)])
        output_shard, inner_shard = both[:, :head_cols].T, both[:, head_cols:]

        last_b = flip(joined(part_b(0, 1), far_b[1]).astype(low), "y")
        outer_shard = joined(part_b(0, 0), far_b[0], last_b).T
    else:
        outer_shard = scatter(outer_weight_grad, whole, hidden_cols).T
        inner_shard = scatter(inner_weight_grad, whole, hidden_cols)
        output_shard = scatter(output_weight_grad, whole, head_cols).T
        qkv_shard = scatter(qkv_weight_grad, ("dp",), 3 * head_cols)
        summed = lax.psum(local, ("dp", "tensor"))
    rows = [summed[at] for at in range(8)]
    return (
        layer_output,
        input_gradient,
        qkv_shard[:, :head_cols],
        rows[0],
        qkv_shard[:, head_cols : 2 * head_cols],
        qkv_shard[:, 2 * head_cols :],
        rows[1],
        output_shard,
        rows[2],
        rows[3],
        rows[4],
        inner_shard,
        summed[8:12].reshape(-1),
        outer_shard,
        rows[5],
        rows[6],
        rows[7],
    )


def solution(mesh):
    placed = (
        P(("dp", "tensor"), None),
        P("dp", "tensor"),
        P(),
        P("dp", "tensor"),
        P("dp", "tensor"),
        P(),
        P("tensor", "dp"),
        P(),
        P(),
        P(),
        P("dp", "tensor"),
        P(),
        P("tensor", "dp"),
        P(),
        P(),
        P(),
        P("dp", None),
        P("dp"),
        P(("dp", "tensor"), None),
    )
    return jax.shard_map(
        layer_on_device,
        mesh=mesh,
        in_specs=placed,
        out_specs=(
            P(("dp", "tensor"), None),
            P(("dp", "tensor"), None),
            P("dp", "tensor"),
            P(),
            P("dp", "tensor"),
            P("dp", "tensor"),
            P(),
            P("tensor", "dp"),
            P(),
            P(),
            P(),
            P("dp", "tensor"),
            P(),
            P("tensor", "dp"),
            P(),
            P(),
            P(),
        ),
        check_vma=False,
    )
```

```python
import jax
import jax.numpy as jnp
from jax import lax
from jax.experimental import pallas as pl
from jax.experimental.pallas import tpu as pltpu
from jax.sharding import PartitionSpec as P

HEAD_DIM = 64


norm_epsilon = 1e-12
masked_score = -1e30


def normalize(matrix, gain, shift):
    center = matrix - jnp.mean(matrix, axis=-1, keepdims=True)
    spread = jnp.mean(center * center, axis=-1, keepdims=True)
    return center * lax.rsqrt(spread + norm_epsilon) * gain + shift


LOG2_E = 1.4426950408889634
QUERY_ROWS = 256


def vmem(mebibytes):
    return pltpu.CompilerParams(vmem_limit_bytes=mebibytes << 20)


def two_heads(rows):
    lane = lax.broadcasted_iota(jnp.int32, rows.shape, 1)
    zero = jnp.zeros_like(rows)
    return jnp.concatenate(
        [jnp.where(lane < HEAD_DIM, rows, zero), jnp.where(lane < HEAD_DIM, zero, rows)], axis=0
    )


def pick_heads(columns):
    count = columns.shape[1] // 2
    row = lax.broadcasted_iota(jnp.int32, (columns.shape[0], count), 0)
    return jnp.where(row < HEAD_DIM, columns[:, :count], columns[:, count:]).T


def masked_scores(keys, queries_two, key_marks, query_marks, first_row):
    scores = lax.dot_general(
        keys, queries_two, (((1,), (1,)), ((), ())), preferred_element_type=jnp.float32
    ) * (0.125 * LOG2_E)
    count = queries_two.shape[0] // 2
    length = keys.shape[0]
    query_two = jnp.concatenate([query_marks, query_marks], axis=1)
    marks = jnp.concatenate([key_marks] * (2 * count // key_marks.shape[1]), axis=1)
    allowed = marks == query_two
    pieces = []
    for start in range(0, length, count):
        part = allowed[start : start + count]
        if start == first_row:
            row = lax.broadcasted_iota(jnp.int32, (count, 2 * count), 0)
            column = lax.broadcasted_iota(jnp.int32, (count, 2 * count), 1)
            part = part | (row == jnp.where(column < count, column, column - count))
        pieces.append(jnp.where(part, scores[start : start + count], masked_score))
    return jnp.concatenate(pieces, axis=0)


def forward_body(
    query_ref, key_ref, value_ref, key_marks_ref, query_marks_ref, own_ref, other_ref, lse_ref
):
    length = key_ref.shape[0]
    keys = key_ref[...]
    values_t = value_ref[...].T
    for first_row in range(0, length, QUERY_ROWS):
        rows = pl.ds(first_row, QUERY_ROWS)
        scores = masked_scores(
            keys,
            two_heads(query_ref[rows, :]),
            key_marks_ref[...],
            query_marks_ref[0, :, rows],
            first_row,
        )
        largest = jnp.max(scores, axis=0, keepdims=True)
        powers = jnp.exp2(scores - largest)
        totals = jnp.sum(powers, axis=0, keepdims=True)
        product = lax.dot_general(
            values_t,
            powers.astype(jnp.bfloat16),
            (((1,), (0,)), ((), ())),
            preferred_element_type=jnp.float32,
        )
        target = own_ref if first_row < length // 2 else other_ref
        target[pl.ds(first_row % (length // 2), QUERY_ROWS), :] = pick_heads(
            product * (1.0 / totals)
        ).astype(jnp.bfloat16)
        lse_ref[0, 0, :, pl.ds(2 * first_row, 2 * QUERY_ROWS)] = largest + jnp.log2(totals)


def backward_body(
    query_ref, key_ref, value_ref, own_ref, far_ref, key_marks_ref, query_marks_ref, lse_ref, out_ref,
    key_sum, value_sum,
):
    length = key_ref.shape[0]
    width = out_ref.shape[1] // 3
    low = jnp.bfloat16
    keys = key_ref[...]
    values = value_ref[...]
    keys_t = keys.T
    column = pl.multiple_of(pl.program_id(1) * 2 * HEAD_DIM, 2 * HEAD_DIM)
    for first_row in range(0, length, QUERY_ROWS):
        rows = pl.ds(first_row, QUERY_ROWS)
        queries_two = two_heads(query_ref[rows, :])
        grad_ref = own_ref if first_row < length // 2 else far_ref
        grads_two = two_heads(grad_ref[pl.ds(first_row % (length // 2), QUERY_ROWS), :])
        scores = masked_scores(
            keys, queries_two, key_marks_ref[...], query_marks_ref[0, :, rows], first_row
        )
        probs = jnp.exp2(scores - lse_ref[0, 0, :, pl.ds(2 * first_row, 2 * QUERY_ROWS)])
        d_probs = lax.dot_general(
            values, grads_two, (((1,), (1,)), ((), ())), preferred_element_type=jnp.float32
        )
        inner = jnp.sum(probs * d_probs, axis=0, keepdims=True)
        d_scores = (probs * (d_probs - inner)).astype(low)
        value_part = lax.dot_general(
            probs.astype(low), grads_two, (((1,), (0,)), ((), ())),
            preferred_element_type=jnp.float32,
        )
        key_part = lax.dot_general(
            d_scores, queries_two, (((1,), (0,)), ((), ())), preferred_element_type=jnp.float32
        )
        if first_row == 0:
            value_sum[...] = value_part
            key_sum[...] = key_part
        else:
            value_sum[...] += value_part
            key_sum[...] += key_part
        query_part = lax.dot_general(
            keys_t, d_scores, (((1,), (0,)), ((), ())), preferred_element_type=jnp.float32
        )
        out_ref[rows, pl.ds(column, 2 * HEAD_DIM)] = (pick_heads(query_part) * 0.125).astype(low)
    out_ref[:, pl.ds(column + width, 2 * HEAD_DIM)] = (key_sum[...] * 0.125).astype(low)
    out_ref[:, pl.ds(column + 2 * width, 2 * HEAD_DIM)] = value_sum[...].astype(low)


def attention_marks(segments, valid_length, shard_index):
    length = segments.shape[1]
    positions = jnp.arange(length, dtype=jnp.int32)
    key_marks = jnp.where(positions[None, :] < valid_length[:, None], segments, -1)

    def own_first(marks):
        return jnp.concatenate(
            own_half_first(marks[:, : length // 2], marks[:, length // 2 :], shard_index), axis=1
        )

    key_marks = jnp.broadcast_to(own_first(key_marks).reshape(-1, 1), (length, 128))
    return key_marks, own_first(segments).reshape(1, 1, length)


def pair_specs(length, pairs, blocks):
    return [
        pl.BlockSpec((length, 2 * HEAD_DIM), lambda s, p, at=at: (s, at * pairs + p))
        for at in blocks
    ]


def attend_forward(qkv, key_marks, query_marks):
    seq_count, _, length = query_marks.shape
    pairs = qkv.shape[1] // (6 * HEAD_DIM)
    return pl.pallas_call(
        forward_body,
        compiler_params=vmem(24),
        out_shape=(
            jax.ShapeDtypeStruct((qkv.shape[0] // 2, qkv.shape[1] // 3), jnp.bfloat16),
            jax.ShapeDtypeStruct((qkv.shape[0] // 2, qkv.shape[1] // 3), jnp.bfloat16),
            jax.ShapeDtypeStruct((seq_count, pairs, 1, 2 * length), jnp.float32),
        ),
        grid=(seq_count, pairs),
        in_specs=pair_specs(length, pairs, (0, 1, 2))
        + [
            pl.BlockSpec((length, 128), lambda s, p: (s, 0)),
            pl.BlockSpec((1, 1, length), lambda s, p: (s, 0, 0)),
        ],
        out_specs=(
            pl.BlockSpec((length // 2, 2 * HEAD_DIM), lambda s, p: (s, p)),
            pl.BlockSpec((length // 2, 2 * HEAD_DIM), lambda s, p: (s, p)),
            pl.BlockSpec((1, 1, 1, 2 * length), lambda s, p: (s, p, 0, 0)),
        ),
    )(qkv, qkv, qkv, key_marks, query_marks)


def attend_backward(qkv, own_grad, far_grad, key_marks, query_marks, lse):
    seq_count, _, length = query_marks.shape
    pairs = qkv.shape[1] // (6 * HEAD_DIM)
    return pl.pallas_call(
        backward_body,
        compiler_params=vmem(32),
        out_shape=jax.ShapeDtypeStruct(qkv.shape, jnp.bfloat16),
        grid=(seq_count, pairs),
        in_specs=pair_specs(length, pairs, (0, 1, 2))
        + [pl.BlockSpec((length // 2, 2 * HEAD_DIM), lambda s, p: (s, p))] * 2
        + [
            pl.BlockSpec((length, 128), lambda s, p: (s, 0)),
            pl.BlockSpec((1, 1, length), lambda s, p: (s, 0, 0)),
            pl.BlockSpec((1, 1, 1, 2 * length), lambda s, p: (s, p, 0, 0)),
        ],
        out_specs=pl.BlockSpec((length, qkv.shape[1]), lambda s, p: (s, 0)),
        scratch_shapes=[pltpu.VMEM((length, 2 * HEAD_DIM), jnp.float32)] * 2,
    )(qkv, qkv, qkv, own_grad, far_grad, key_marks, query_marks, lse)


def slope_and_gelu(inner):
    rise = 0.5 * (1.0 + lax.erf(inner * 0.7071067811865476))
    density = jnp.exp(-0.5 * inner * inner) * 0.3989422804014327
    return inner * rise, rise + inner * density


def norm_backward(matrix, gain, grad):
    center = matrix - jnp.mean(matrix, axis=-1, keepdims=True)
    spread = jnp.mean(center * center, axis=-1, keepdims=True)
    scale = lax.rsqrt(spread + norm_epsilon)
    normed = center * scale
    d_normed = grad * gain
    pulled = scale * (
        d_normed
        - jnp.mean(d_normed, axis=-1, keepdims=True)
        - normed * jnp.mean(d_normed * normed, axis=-1, keepdims=True)
    )
    return (
        pulled,
        jnp.sum(grad * normed, axis=0),
        jnp.sum(grad, axis=0),
    )


def own_half_first(mine, other, shard_index):
    first = shard_index == 0
    return jnp.where(first, mine, other), jnp.where(first, other, mine)


def mix(left, right, dims):
    return lax.dot_general(left, right, (dims, ((), ())), preferred_element_type=jnp.float32)


def flip(array, bit):
    step = {"x": 1, "core": 2, "y": 4, "xy": 5}[bit]
    return lax.ppermute(array, ("dp", "tensor"), [(i, i ^ step) for i in range(32)])


def turn(array, shift):
    return lax.ppermute(array, "dp", [(i, (i + 4 * shift) % 16) for i in range(16)])


def after(array, done):
    return lax.optimization_barrier((array, done))[0]


def whereabouts():
    index = lax.axis_index("dp")
    return dict(z=index // 4, y=(index // 2) % 2, core=index % 2, x=lax.axis_index("tensor"))


def around_z(block):
    return jnp.stack([block] + [turn(block, shift) for shift in (1, 2, 3)])


def assemble(pieces, place, parts, in_rotation):
    keys = sorted(pieces)
    many_x = 2 if in_rotation or any(key[1] for key in keys) else 1
    rows = pieces[keys[0]].shape[1]
    outs = [
        jax.ShapeDtypeStruct((4, 2, 2, rows, many_x * cols), jnp.bfloat16) for _, cols in parts
    ]

    def put(spot, targets, block, core_off, x_off, y_off):
        core = (spot[2] + core_off) % 2
        y = (spot[1] + y_off) % 2
        for target, (start, cols) in zip(targets, parts):
            target[0, y, core, :, x_off * cols : (x_off + 1) * cols] = block[
                :, start : start + cols
            ]

    def body(spot, *refs):
        sources, targets = refs[: len(keys)], refs[len(keys) :]
        if not in_rotation:
            for number, (core_off, x_off, y_off) in enumerate(keys):
                put(spot, targets, sources[number][0], core_off, x_off, y_off)
            return
        for number, (core_off, shift) in enumerate(keys):

            @pl.when(pl.program_id(0) == shift)
            def _():
                for plane in range(4):
                    block = sources[number][plane]
                    put(spot, targets, block, core_off, plane // 2, plane % 2)

    spot = jnp.stack([place[name] for name in ("z", "y", "core")]).astype(jnp.int32)
    shape = pieces[keys[0]].shape
    if in_rotation:
        piece_spec = pl.BlockSpec(shape, lambda i, spot: (0, 0, 0))
    else:
        piece_spec = pl.BlockSpec((1,) + shape[1:], lambda i, spot: (i, 0, 0))
    results = pl.pallas_call(
        body,
        compiler_params=vmem(16),
        out_shape=outs,
        grid_spec=pltpu.PrefetchScalarGridSpec(
            num_scalar_prefetch=1,
            grid=(4,),
            in_specs=[piece_spec] * len(keys),
            out_specs=[
                pl.BlockSpec(
                    (1,) + out.shape[1:], lambda i, spot: ((spot[0] + 4 - i) % 4, 0, 0, 0, 0)
                )
                for out in outs
            ],
        ),
    )(spot, *[pieces[key] for key in keys])
    return [result.reshape(16 * rows, result.shape[-1]) for result in results]


def side_by_side(*arrays):
    def body(*refs):
        at = 0
        for ref in refs[:-1]:
            refs[-1][:, at : at + ref.shape[1]] = ref[...]
            at += ref.shape[1]

    cols = sum(array.shape[1] for array in arrays)
    return pl.pallas_call(
        body,
        compiler_params=vmem(4),
        out_shape=jax.ShapeDtypeStruct((arrays[0].shape[0], cols), arrays[0].dtype),
    )(*arrays)


def project(own, other, pieces, place, bias):
    rows, width = own.shape
    keys = sorted(pieces)
    cols = pieces[keys[0]].shape[2]
    high = width // 16

    def body(spot, own_ref, other_ref, bias_ref, *refs):
        sources, weight_ref, out_ref = refs[:-2], refs[-2], refs[-1]

        @pl.when(pl.program_id(0) == 0)
        def _():
            for ref, (core_off, _, y_off) in zip(sources, keys):
                core, y = (spot[2] + core_off) % 2, (spot[1] + y_off) % 2
                for shift in range(4):
                    weight_ref[(spot[0] + 4 - shift) % 4, y, core] = ref[shift]

        weight = weight_ref[...].reshape(width, cols)

        def write(ref):
            product = jnp.dot(ref[...], weight, preferred_element_type=jnp.float32)
            out_ref[...] = (product + bias_ref[...]).astype(jnp.bfloat16)

        pl.when(pl.program_id(0) < 2)(lambda: write(own_ref))
        pl.when(pl.program_id(0) >= 2)(lambda: write(other_ref))

    spot = jnp.stack([place["z"], place["y"], place["core"]]).astype(jnp.int32)
    weight, out = pl.pallas_call(
        body,
        compiler_params=vmem(16),
        out_shape=[
            jax.ShapeDtypeStruct((4, 2, 2, high, cols), jnp.bfloat16),
            jax.ShapeDtypeStruct((2 * rows, cols), jnp.bfloat16),
        ],
        grid_spec=pltpu.PrefetchScalarGridSpec(
            num_scalar_prefetch=1,
            grid=(4,),
            in_specs=[
                pl.BlockSpec((rows // 2, width), lambda i, spot: (jnp.minimum(i, 1), 0)),
                pl.BlockSpec((rows // 2, width), lambda i, spot: (jnp.maximum(i - 2, 0), 0)),
                pl.BlockSpec((1, cols), lambda i, spot: (0, 0)),
            ]
            + [pl.BlockSpec((4, high, cols), lambda i, spot: (0, 0, 0))] * len(keys),
            out_specs=[
                pl.BlockSpec((4, 2, 2, high, cols), lambda i, spot: (0, 0, 0, 0, 0)),
                pl.BlockSpec((rows // 2, cols), lambda i, spot: (i, 0)),
            ],
        ),
    )(spot, own, other, bias.reshape(1, cols), *[pieces[key] for key in keys])
    return weight.reshape(width, cols), out


def joined(first, *others):
    total = first.astype(jnp.float32)
    for other in others:
        total = total + other.astype(jnp.float32)
    return total


def other_cores(grad, place):
    blocks = grad.reshape(4, 2, 2, grad.shape[0] // 16, grad.shape[1])
    send = lax.dynamic_index_in_dim(blocks, 1 - place["core"], 2, keepdims=False)
    return blocks, flip(send, "core")


def combine(pairs, place, many_x, z_apart, cut=None):
    rows = pairs[0][0].shape[3]
    widths = [blocks.shape[4] // many_x for blocks, _ in pairs]
    count = len(pairs)

    def body(spot, *refs):
        outs = refs[2 * count :]
        for y_off in range(2):
            y = (spot[1] + y_off) % 2
            at = 0
            for number, cols in enumerate(widths):
                blocks, far = refs[2 * number], refs[2 * number + 1]
                total = blocks[0, y, 0].astype(jnp.float32) + far[0, y].astype(jnp.float32)
                if z_apart:
                    for shift in range(4):

                        @pl.when(pl.program_id(0) == shift)
                        def _():
                            outs[shift][y_off] = total.astype(outs[shift].dtype)

                    continue
                for x_off in range(many_x):
                    place_at = x_off * 2 + y_off
                    part = total[:, x_off * cols : (x_off + 1) * cols]
                    for out, low_end, high_end in ranges(place_at, outs):
                        start, stop = max(at, low_end), min(at + cols, high_end)
                        if start < stop:
                            out[0, :, start - low_end : stop - low_end] = part[
                                :, start - at : stop - at
                            ].astype(out.dtype)
                at += cols

    def ranges(place_at, outs):
        if cut is None:
            return [(outs[place_at], 0, sum(widths))]
        return [
            (outs[2 * place_at], 0, cut),
            (outs[2 * place_at + 1], cut, sum(widths)),
        ]

    spot = jnp.stack([place[name] for name in ("z", "y", "core")]).astype(jnp.int32)
    in_specs = []
    for blocks, _ in pairs:
        n = blocks.shape[4]
        in_specs.append(
            pl.BlockSpec(
                (1, 2, 1, rows, n), lambda i, spot: ((spot[0] + i) % 4, 0, spot[2], 0, 0)
            )
        )
        in_specs.append(
            pl.BlockSpec((1, 2, rows, n), lambda i, spot: ((spot[0] + i) % 4, 0, 0, 0))
        )
    if z_apart:
        shapes = [(2, rows, pairs[0][0].shape[4])] * 4
        out_specs = [pl.BlockSpec(shapes[0], lambda i, spot: (0, 0, 0))] * 4
    else:
        ends = [sum(widths)] if cut is None else [cut, sum(widths) - cut]
        shapes = [(4, rows, cols) for _ in range(2 * many_x) for cols in ends]
        out_specs = [pl.BlockSpec((1,) + shape[1:], lambda i, spot: (i, 0, 0)) for shape in shapes]
    wide = 1 if cut is None else 2
    return pl.pallas_call(
        body,
        compiler_params=vmem(16),
        out_shape=[
            jax.ShapeDtypeStruct(shape, jnp.bfloat16 if at >= wide else jnp.float32)
            for at, shape in enumerate(shapes)
        ],
        grid_spec=pltpu.PrefetchScalarGridSpec(
            num_scalar_prefetch=1, grid=(4,), in_specs=in_specs, out_specs=out_specs
        ),
    )(spot, *[array for pair in pairs for array in pair])


def over_z(groups):
    flat = [array for group in groups for array in group]
    rows = flat[0].shape[1]
    cols = sum(group[0].shape[2] for group in groups)

    def body(*refs):
        outs = refs[len(flat) :]
        for shift in range(4):

            @pl.when(pl.program_id(0) == shift)
            def _():
                used = at = 0
                for group in groups:
                    total = joined(*[ref[0] for ref in refs[used : used + len(group)]])
                    used += len(group)
                    outs[shift][:, at : at + total.shape[1]] = total.astype(outs[shift].dtype)
                    at += total.shape[1]

    parts = pl.pallas_call(
        body,
        compiler_params=vmem(8),
        out_shape=[
            jax.ShapeDtypeStruct((rows, cols), jnp.bfloat16 if shift else jnp.float32)
            for shift in range(4)
        ],
        grid=(4,),
        in_specs=[pl.BlockSpec((1,) + array.shape[1:], lambda i: (i, 0, 0)) for array in flat],
        out_specs=[pl.BlockSpec((rows, cols), lambda i: (0, 0))] * 4,
    )(*flat)
    arrived = [turn(parts[shift], shift) for shift in (1, 2, 3)]
    return joined(parts[0], *arrived)


def pack_sums(shard_index, bias_sums, vectors, inner_sums):
    width = vectors[0].shape[0]
    half = width // 2
    wide = inner_sums.shape[0] // 2

    def body(spot, bias_ref, *refs):
        out = refs[-1]
        first = spot[0] == 0
        out[...] = jnp.zeros(out.shape, jnp.float32)
        empty = jnp.zeros((1, half), jnp.float32)
        for row, at in enumerate((0, 2)):
            part = bias_ref[at * half : (at + 1) * half].reshape(1, half)
            out[row : row + 1, :] = jnp.concatenate(
                [jnp.where(first, part, empty), jnp.where(first, empty, part)], axis=1
            )
        for row, ref in enumerate(refs[:-2]):
            out[2 + row : 3 + row, :] = ref[...].reshape(1, width)
        inner = refs[-2][...].reshape(1, 2 * wide)
        mine, far = inner[:, :wide], inner[:, wide:]
        ordered = (jnp.where(first, mine, far), jnp.where(first, far, mine))
        row = 2 + len(refs[:-2])
        for part in ordered:
            for start in range(0, wide, width):
                out[row : row + 1, :] = part[:, start : start + width]
                row += 1

    return pl.pallas_call(
        body,
        compiler_params=vmem(4),
        out_shape=jax.ShapeDtypeStruct((16, width), jnp.float32),
        in_specs=[pl.BlockSpec(memory_space=pltpu.SMEM)]
        + [pl.BlockSpec(memory_space=pltpu.VMEM)] * (2 + len(vectors)),
    )(shard_index.reshape(1).astype(jnp.int32), bias_sums, *vectors, inner_sums)


def layer_on_device(
    tokens,
    query_weight,
    query_bias,
    key_weight,
    value_weight,
    value_bias,
    output_weight,
    output_bias,
    first_gain,
    first_shift,
    inner_weight,
    inner_bias,
    outer_weight,
    outer_bias,
    second_gain,
    second_shift,
    segments,
    valid_length,
    cotangent,
):
    low = jnp.bfloat16
    whole = ("tensor", "dp")
    by_links = lax.axis_size("dp") == 16
    place = whereabouts()
    own_rows, width = tokens.shape
    head_cols = query_weight.shape[1]
    hidden_cols = inner_weight.shape[1]
    shard_index = lax.axis_index("tensor")

    other_tokens = flip(tokens, "x")
    packed_qkv = side_by_side(query_weight, key_weight, value_weight)
    packed_in = side_by_side(output_weight.T, inner_weight)
    packed_out = outer_weight.T
    if by_links:
        near_q = around_z(packed_qkv)
        far_q = flip(near_q, "y")
        pieces_q = {
            (0, 0, 0): near_q,
            (0, 0, 1): far_q,
            (1, 0, 0): flip(near_q, "core"),
            (1, 0, 1): flip(far_q, "core"),
        }
        near_a = around_z(after(packed_in, near_q))
        square = jnp.stack([packed_out] + [flip(packed_out, bit) for bit in ("y", "x", "xy")])
        square_z = [square] + [turn(after(square, near_a), shift) for shift in (1, 2, 3)]
        plane_a = [near_a] + [flip(near_a, bit) for bit in ("y", "x")]
    else:
        near_a = None
        full_qkv = lax.all_gather(packed_qkv, "dp", axis=0, tiled=True)
        gathered = lax.all_gather(packed_in, whole, axis=0, tiled=True)
        gathered = gathered.reshape(2, width, head_cols + hidden_cols)
        mine, far = own_half_first(gathered[0], gathered[1], shard_index)
        full_output = jnp.concatenate([mine[:, :head_cols], far[:, :head_cols]], axis=1)
        full_inner = jnp.concatenate([mine[:, head_cols:], far[:, head_cols:]], axis=1)
        gathered = lax.all_gather(packed_out, whole, axis=0, tiled=True)
        gathered = gathered.reshape(2, width, hidden_cols)
        full_outer = jnp.concatenate(
            own_half_first(gathered[0], gathered[1], shard_index), axis=1
        )

    bias_query = lax.dynamic_slice_in_dim(query_bias, shard_index * head_cols, head_cols)
    bias_value = lax.dynamic_slice_in_dim(value_bias, shard_index * head_cols, head_cols)
    bias_qkv = jnp.concatenate([bias_query, jnp.zeros_like(bias_query), bias_value])
    if by_links:
        full_qkv, qkv = project(tokens, other_tokens, pieces_q, place, bias_qkv)
    else:
        rows_all = jnp.concatenate([tokens, other_tokens], axis=0)
        qkv = (mix(rows_all, full_qkv, ((1,), (0,))) + bias_qkv).astype(low)
    key_marks, query_marks = attention_marks(segments, valid_length, shard_index)
    own_context, other_context, log_totals = attend_forward(qkv, key_marks, query_marks)
    far_context = flip(other_context, "x")
    if by_links:
        plane_a.append(flip(plane_a[2], "y"))
        pieces = {(0, at // 2, at % 2): piece for at, piece in enumerate(plane_a)}
        pieces.update({(1,) + key[1:]: flip(piece, "core") for key, piece in pieces.items()})
        full_output, full_inner = assemble(
            pieces, place, [(0, head_cols), (head_cols, hidden_cols)], False
        )
        pieces = {(0, shift): piece for shift, piece in enumerate(square_z)}
        pieces.update({(1, shift): flip(piece, "core") for shift, piece in enumerate(square_z)})
        (full_outer,) = assemble(pieces, place, [(0, hidden_cols)], True)
    own_rows_context = jnp.concatenate([own_context, far_context], axis=1)
    attended = mix(own_rows_context, full_output, ((1,), (1,)))
    first_sum = tokens.astype(jnp.float32) + attended + output_bias
    hidden = normalize(first_sum, first_gain, first_shift)
    hidden_low = hidden.astype(low)
    bias_inner = jnp.concatenate(
        own_half_first(inner_bias[:hidden_cols], inner_bias[hidden_cols:], shard_index)
    )
    inner = mix(hidden_low, full_inner, ((1,), (0,))) + bias_inner
    value, slope = slope_and_gelu(inner)
    activated = value.astype(low)
    second_sum = hidden + mix(activated, full_outer, ((1,), (1,))) + outer_bias
    layer_output = normalize(second_sum, second_gain, second_shift).astype(low)
    d_second, second_gain_grad, second_shift_grad = norm_backward(
        second_sum, second_gain, cotangent.astype(jnp.float32)
    )
    outer_bias_grad = jnp.sum(d_second, axis=0)
    d_outer = d_second.astype(low)
    outer_weight_grad = mix(d_outer, activated, ((0,), (0,))).astype(low)
    held_d_outer = after(d_outer, outer_weight_grad)
    d_activated = mix(held_d_outer, full_outer, ((1,), (0,)))
    d_inner = (d_activated * slope).astype(low)
    inner_weight_grad = mix(hidden_low, d_inner, ((0,), (0,))).astype(low)
    inner_bias_grad = jnp.sum(d_inner, axis=0, dtype=jnp.float32)
    through = mix(d_inner, full_inner, ((1,), (1,)))
    d_hidden = d_second + through
    d_first, first_gain_grad, first_shift_grad = norm_backward(first_sum, first_gain, d_hidden)
    output_bias_grad = jnp.sum(d_first, axis=0)
    d_attended = d_first.astype(low)
    output_weight_grad = mix(d_attended, own_rows_context, ((0,), (0,))).astype(low)
    d_own_context = mix(d_attended, full_output, ((1,), (0,))).astype(low)
    far_d_context = flip(d_own_context[:, head_cols:], "x")
    if by_links:
        square_b = combine([other_cores(outer_weight_grad, place)], place, 2, True)
        turned_b = [square_b[0]] + [turn(square_b[shift], shift) for shift in (1, 2, 3)]
        plane_a = combine(
            [other_cores(output_weight_grad, place), other_cores(inner_weight_grad, place)],
            place,
            2,
            False,
            cut=1024,
        )
        far_a = (flip(plane_a[6], "y"), flip(plane_a[7], "x"))
        near_a = (flip(plane_a[2], "y"), flip(plane_a[5], "x"))
    d_qkv = attend_backward(
        qkv, d_own_context, far_d_context, key_marks, query_marks, log_totals)
    if by_links:
        late_a = (
            flip(joined(plane_a[4], far_a[0]).astype(low), "x"),
            flip(joined(plane_a[3], far_a[1]).astype(low), "y"),
        )
    qkv_weight_grad = (
        mix(tokens, d_qkv[:own_rows], ((0,), (0,)))
        + mix(other_tokens, d_qkv[own_rows:], ((0,), (0,)))
    ).astype(low)
    held_d_qkv = after(d_qkv, qkv_weight_grad)
    partial_input = mix(held_d_qkv, full_qkv, ((1,), (1,)))
    if by_links:

        def part_b(x_off, y_off=None):
            rows = slice(None) if y_off is None else y_off
            columns = slice(x_off * hidden_cols, (x_off + 1) * hidden_cols)
            return joined(*[rows_b[rows, :, columns] for rows_b in turned_b])

        far_b = flip(part_b(1).astype(low), "x")
    far_input = flip(partial_input[own_rows:].astype(low), "x")
    input_gradient = d_first + partial_input[:own_rows] + far_input.astype(jnp.float32)

    def scatter(grad, axes, cols):
        if grad.shape[1] > cols:
            grad = jnp.concatenate(
                own_half_first(grad[:, :cols], grad[:, cols:], shard_index), axis=0
            )
        return lax.psum_scatter(grad, axes, scatter_dimension=0, tiled=True).astype(jnp.float32)

    bias_local = jnp.sum(d_qkv, axis=0, dtype=jnp.float32)
    local = pack_sums(
        shard_index,
        bias_local,
        [
            output_bias_grad,
            first_gain_grad,
            first_shift_grad,
            outer_bias_grad,
            second_gain_grad,
            second_shift_grad,
        ],
        inner_bias_grad,
    )
    if by_links:
        local = local + flip(local, "core")
        plane_q = combine([other_cores(qkv_weight_grad, place)], place, 1, False)
        far_q = flip(plane_q[1], "y")
        met = [flip(local, bit) for bit in ("x", "y", "xy")]
        local = (local + met[0]) + (met[1] + met[2])
        qkv_shard = over_z([(plane_q[0], far_q)])
        turned = [turn(local, shift) for shift in (1, 2, 3)]
        summed = (local + turned[1]) + (turned[0] + turned[2])
        both = over_z([(plane_a[at], near_a[at], late_a[at]) for at in range(2)])
        output_shard, inner_shard = both[:, :head_cols].T, both[:, head_cols:]

        last_b = flip(joined(part_b(0, 1), far_b[1]).astype(low), "y")
        outer_shard = joined(part_b(0, 0), far_b[0], last_b).T
    else:
        outer_shard = scatter(outer_weight_grad, whole, hidden_cols).T
        inner_shard = scatter(inner_weight_grad, whole, hidden_cols)
        output_shard = scatter(output_weight_grad, whole, head_cols).T
        qkv_shard = scatter(qkv_weight_grad, ("dp",), 3 * head_cols)
        summed = lax.psum(local, ("dp", "tensor"))
    rows = [summed[at] for at in range(8)]
    return (
        layer_output,
        input_gradient,
        qkv_shard[:, :head_cols],
        rows[0],
        qkv_shard[:, head_cols : 2 * head_cols],
        qkv_shard[:, 2 * head_cols :],
        rows[1],
        output_shard,
        rows[2],
        rows[3],
        rows[4],
        inner_shard,
        summed[8:12].reshape(-1),
        outer_shard,
        rows[5],
        rows[6],
        rows[7],
    )


def solution(mesh):
    placed = (
        P(("dp", "tensor"), None),
        P("dp", "tensor"),
        P(),
        P("dp", "tensor"),
        P("dp", "tensor"),
        P(),
        P("tensor", "dp"),
        P(),
        P(),
        P(),
        P("dp", "tensor"),
        P(),
        P("tensor", "dp"),
        P(),
        P(),
        P(),
        P("dp", None),
        P("dp"),
        P(("dp", "tensor"), None),
    )
    return jax.shard_map(
        layer_on_device,
        mesh=mesh,
        in_specs=placed,
        out_specs=(
            P(("dp", "tensor"), None),
            P(("dp", "tensor"), None),
            P("dp", "tensor"),
            P(),
            P("dp", "tensor"),
            P("dp", "tensor"),
            P(),
            P("tensor", "dp"),
            P(),
            P(),
            P(),
            P("dp", "tensor"),
            P(),
            P("tensor", "dp"),
            P(),
            P(),
            P(),
        ),
        check_vma=False,
    )
```
